256 devices in a mesh: seq: 64 (over z, x, core), tp: 4 (over y).
Axes of the slice: x: 4, y: 4, z: 8, core: 2. Of those that a mesh axis runs over, the one named last changes fastest.
Arguments:
- tokens: bfloat16 [32768, 3072], P('seq', 'tp')
- norm_gain: float32 [3072], replicated, may hold values from 0.1 to 1.9
- w_query: bfloat16 [3072, 1536], P(None, 'tp'), as said below
- w_key: bfloat16 [3072, 1536], P(None, 'tp'), as said below
- w_value: bfloat16 [3072, 1536], P(None, 'tp'), may hold values from -0.109375 to 0.109375
- w_out: bfloat16 [1536, 3072], P('tp'), may hold values from -0.625 to 0.625
- final_gain: float32 [3072], P('tp'), may hold values from 0.1 to 1.9
- w_vocab: bfloat16 [3072, 32064], P('tp', 'seq'), may hold values from -0.3125 to 0.3125
- segment_ids: int32 [32768], P('seq'), may hold values from -1 to 7, as said below
- prompt_lengths: int32 [8], replicated, may hold values from 1 to 8192, as said below
- request_slots: int32 [128], replicated, may hold values from 0 to 32511, as said below
Outputs:
- kv_cache: bfloat16 [16, 32768, 192], P('tp', 'seq')
- hidden: bfloat16 [32768, 3072], P('seq', 'tp')
- hidden_norm: float32 [128], replicated
- top_logit: float32 [128], replicated
The draws below stay inside these ranges and needn't reach their ends.
Inputs may be any that keep to these rules, and one draw needn't show every extreme that they name: `segment_ids`: prompts 0 to 7 fill the slots in order from slot 0, prompt p on prompt_lengths[p] consecutive slots; all later slots are -1. `prompt_lengths`: they sum to 32512; the last prompt has exactly 8192 slots, and no prompt has more. `request_slots`: request r names a slot of prompt r // 16; the last request of each prompt names that prompt's final slot. `w_query`: Real-valued weights. `w_key`: Real-valued weights.
All inputs are finite; a program needn't handle non-finite values.
Results may differ from the reference program's by a relative error of at most 0.0095.
Values may be sent and summed in bfloat16 or wider, within the bound.
A program may use at most 128 MiB of HBM per device.

```python
import math
import jax
import jax.numpy as jnp
from jax import lax

D = 3072
HEADS = 16
HD = 96
VOCAB = 32064
PROMPTS = 8
REQ_PER = 16
TOK_DEV = 512
TOKENS = 32768
MAXLEN = 8192
REQS = 128
N_TP = 4


def prompt_plan(key):
    base = jax.random.fold_in(key, 101)
    weights = jax.random.randint(jax.random.fold_in(base, 1), (PROMPTS - 1,), 500, 1001)
    remainder = TOKENS - TOK_DEV // 2 - MAXLEN
    others = remainder * weights // jnp.sum(weights)
    others = others.at[PROMPTS - 2].add(remainder - jnp.sum(others))
    order = jax.random.permutation(jax.random.fold_in(base, 2), PROMPTS - 1)
    others = others[order].astype(jnp.int32)
    return jnp.concatenate([others, jnp.full((1,), MAXLEN, jnp.int32)]).astype(jnp.int32)


def draw_prompt_lengths(key, part):
    return prompt_plan(key)


def draw_segment_ids(key, part):
    lengths = prompt_plan(key)
    ends = jnp.cumsum(lengths)
    slots = jnp.arange(TOKENS, dtype=jnp.int32)
    index = jnp.sum((slots[:, None] >= ends[None, :]).astype(jnp.int32), axis=1)
    return jnp.where(index >= PROMPTS, -1, index).astype(jnp.int32)


def draw_request_slots(key, part):
    lengths = prompt_plan(key)
    starts = jnp.cumsum(lengths) - lengths
    offsets = jax.random.randint(jax.random.fold_in(key, 202), (PROMPTS, REQ_PER), 0, lengths[:, None])
    offsets = offsets.at[:, REQ_PER - 1].set(lengths - 1)
    return (starts[:, None] + offsets).reshape(REQS).astype(jnp.int32)


def draw_tokens(key, part):
    column = jnp.arange(D, dtype=jnp.float32) / (D - 1)
    ramp = 0.5 * jnp.exp(column * math.log(4.0))
    values = jax.random.normal(jax.random.fold_in(key, 4), (TOKENS, D), jnp.float32)
    return (values * ramp[None, :]).astype(jnp.bfloat16)


def projection_pair(key):
    first = jax.random.normal(jax.random.fold_in(key, 31), (D, HEADS * HD), jnp.float32) * D ** (-0.5)
    second = jax.random.normal(jax.random.fold_in(key, 32), (D, HEADS * HD), jnp.float32) * D ** (-0.5)
    return (first, second)


def draw_w_query(key, part):
    return projection_pair(key)[0].astype(jnp.bfloat16)


def draw_w_key(key, part):
    return projection_pair(key)[1].astype(jnp.bfloat16)


def shard_levels(own_key, shape, pieces, least, high):
    gain, own = 1.0, jax.random.fold_in(own_key, 6)
    for axis_at, shards_of in pieces:
        heights = jnp.exp(jax.random.uniform(jax.random.fold_in(own, axis_at), (shards_of,), jnp.float32, least / len(pieces), high / len(pieces)))
        gain = gain * jnp.repeat(heights, shape[axis_at] // shards_of).reshape([-1 if axis == axis_at else 1 for axis in range(len(shape))])
    return gain


def centred(stream_key, dims, spread, reach, pieces=(), held_as=jnp.bfloat16):
    loudness = shard_levels(stream_key, dims, pieces, -0.22, 0.18) if pieces else 1.0
    values = jax.random.normal(stream_key, dims, jnp.float32) * spread * loudness
    return jnp.minimum(jnp.maximum(values, -reach), reach).astype(held_as)


def setup_inputs(seed: int = 0) -> dict:
    seeds = jax.random.split(jax.random.key(seed), 12)
    return {
        "tokens": draw_tokens(jax.random.fold_in(seeds[11], 71), 0),
        "norm_gain": jnp.clip(1.0 + 0.18 * jax.random.normal(seeds[1], (D,), jnp.float32), 0.1, 1.9),
        "w_query": draw_w_query(jax.random.fold_in(seeds[11], 71), 0),
        "w_key": draw_w_key(jax.random.fold_in(seeds[11], 71), 0),
        "w_value": centred(seeds[4], (D, HEADS * HD), D ** -0.5, 0.109375, ((1, 4),)),
        "w_out": centred(seeds[5], (HEADS * HD, D), (HEADS * HD // 16) ** -0.5, 0.625, ((0, 4),)),
        "final_gain": jnp.clip(1.0 + 0.18 * jax.random.normal(seeds[6], (D,), jnp.float32), 0.1, 1.9),
        "w_vocab": centred(seeds[7], (D, VOCAB), (D // 9) ** -0.5, 0.3125, ((0, 4), (1, 64))),
        "segment_ids": draw_segment_ids(jax.random.fold_in(seeds[11], 71), 0),
        "prompt_lengths": draw_prompt_lengths(jax.random.fold_in(seeds[11], 71), 0),
        "request_slots": draw_request_slots(jax.random.fold_in(seeds[11], 71), 0),
    }


NEG = -1e+30

def rotate(field, positions):
    middle = HD // 2
    inverse = 10000.0 ** (-(jnp.arange(middle, dtype=jnp.float32) * 2.0 / HD))
    angles = positions.astype(jnp.float32)[:, None] * inverse[None, :]
    cosine = jnp.cos(angles)[:, None, :]
    sine = jnp.sin(angles)[:, None, :]
    first = field[..., :middle]
    second = field[..., middle:]
    return jnp.concatenate([first * cosine - second * sine, second * cosine + first * sine], axis=-1)

def reference(tokens, norm_gain, w_query, w_key, w_value, w_out, final_gain, w_vocab, segment_ids, prompt_lengths, request_slots):
    wide = tokens.astype(jnp.float32)
    normed = (wide * lax.rsqrt(lax.optimization_barrier(jnp.mean(wide * wide, axis=-1, keepdims=True)) + 1e-05) * norm_gain).astype(jnp.bfloat16)
    starts = jnp.cumsum(prompt_lengths) - prompt_lengths
    matches = segment_ids[:, None] == jnp.arange(PROMPTS, dtype=jnp.int32)[None, :]
    first_slot = lax.optimization_barrier(jnp.sum(jnp.where(matches, starts[None, :], 0), axis=1)).astype(jnp.int32)
    slots = jnp.arange(TOKENS, dtype=jnp.int32)
    positions = jnp.where(segment_ids >= 0, slots - first_slot, 0).astype(jnp.int32)
    query = jnp.dot(normed, w_query, preferred_element_type=jnp.float32).reshape(TOKENS, HEADS, HD)
    key = jnp.dot(normed, w_key, preferred_element_type=jnp.float32).reshape(TOKENS, HEADS, HD)
    value = jnp.dot(normed, w_value, preferred_element_type=jnp.float32).reshape(TOKENS, HEADS, HD)
    rot_query = rotate(query, positions).astype(jnp.bfloat16)
    rot_key = rotate(key, positions).astype(jnp.bfloat16)
    paired = jnp.concatenate([rot_key, value.astype(jnp.bfloat16)], axis=-1)
    kv_cache = jnp.transpose(paired, (1, 0, 2))
    marks = jnp.where(segment_ids >= 0, segment_ids + 1, 0).astype(jnp.int32)
    padded_keys = jnp.concatenate([jnp.zeros((MAXLEN, HEADS, 2 * HD), jnp.bfloat16), paired], axis=0)
    padded_marks = jnp.concatenate([jnp.zeros((MAXLEN,), jnp.int32), marks], axis=0)
    scale = HD ** (-0.5)

    def one_block(index):
        begin = (index * TOK_DEV).astype(jnp.int32)
        query_block = lax.dynamic_slice_in_dim(rot_query, begin, TOK_DEV, 0).astype(jnp.float32)
        query_marks = lax.dynamic_slice_in_dim(marks, begin, TOK_DEV, 0)
        key_block = lax.dynamic_slice_in_dim(padded_keys, begin, MAXLEN + TOK_DEV, 0)
        key_marks = lax.dynamic_slice_in_dim(padded_marks, begin, MAXLEN + TOK_DEV, 0)
        keys = key_block[..., :HD].astype(jnp.float32)
        values = key_block[..., HD:].astype(jnp.float32)
        scores = jnp.einsum('qhd,khd->hqk', query_block, keys) * scale
        query_index = jnp.arange(TOK_DEV, dtype=jnp.int32)[:, None]
        key_index = jnp.arange(MAXLEN + TOK_DEV, dtype=jnp.int32)[None, :]
        allowed = (query_marks[:, None] == key_marks[None, :]) & (query_marks[:, None] > 0) & (key_index <= query_index + MAXLEN)
        masked = jnp.where(allowed[None], scores, NEG)
        largest = lax.optimization_barrier(jnp.max(masked, axis=-1))
        weights = jnp.where(allowed[None], jnp.exp(masked - largest[..., None]), 0.0)
        total = lax.optimization_barrier(jnp.sum(weights, axis=-1))
        rounded = lax.optimization_barrier(weights.astype(jnp.bfloat16)).astype(jnp.float32)
        numer = jnp.einsum('hqk,khd->hqd', rounded, values)
        attended = numer / jnp.where(total > 0, total, 1.0)[..., None]
        return jnp.transpose(attended, (1, 0, 2)).astype(jnp.bfloat16)
    blocks = lax.map(one_block, jnp.arange(TOKENS // TOK_DEV, dtype=jnp.int32))
    mixed = blocks.reshape(TOKENS, HEADS * HD)
    group_width = HEADS // N_TP * HD
    summed = jnp.zeros((TOKENS, D), jnp.float32)
    for group in range(N_TP):
        part_cols = mixed[:, group * group_width:(group + 1) * group_width]
        part_rows = w_out[group * group_width:(group + 1) * group_width]
        term = jnp.dot(part_cols, part_rows, preferred_element_type=jnp.float32).astype(jnp.bfloat16)
        summed = summed + lax.optimization_barrier(term).astype(jnp.float32)
    hidden_full = wide + summed
    hidden = hidden_full.astype(jnp.bfloat16)
    request_rows = hidden_full[request_slots]
    hidden_norm = jnp.sqrt(lax.optimization_barrier(jnp.mean(request_rows * request_rows, axis=-1)) + 1e-05)
    scaled_rows = request_rows * final_gain / hidden_norm[:, None]
    logits = jnp.dot(scaled_rows, w_vocab.astype(jnp.float32), precision=lax.Precision.HIGHEST)
    top_logit = lax.optimization_barrier(jnp.max(logits, axis=-1))
    return (kv_cache, hidden, hidden_norm, top_logit)
```

```python
from functools import partial

import jax
import jax.numpy as jnp
from jax import lax
from jax.experimental import pallas as pl
from jax.experimental.pallas import tpu as pltpu
from jax.sharding import PartitionSpec as P

D = 3072
HD = 96
REQS = 128
MESH = pl.DeviceIdType.MESH

NEG = -1e30


def place():
    s = lax.axis_index("seq")
    return s // 8, s % 8, lax.axis_index("tp")


def tail_kernel(
    rows, gain, vocab, norm_out, top_out,
    vpad, buf1, acc1, buf2, chunk, full, part, sq, partr, sqr, mine, buf5, buf6, fin,
    send, recv,
):
    z, p, y = place()

    def peer_z(d):
        return (lax.rem(z + d, 8) * 8 + p, y)

    def peer_p(d):
        return (z * 8 + lax.rem(p + d, 8), y)

    def peer_y(d):
        return (z * 8 + p, lax.rem(y + d, 4))

    barrier = pltpu.get_barrier_semaphore()
    for d in range(1, 8):
        pl.semaphore_signal(barrier, inc=1, device_id=peer_z(d), device_id_type=MESH)
        pl.semaphore_signal(barrier, inc=1, device_id=peer_p(d), device_id_type=MESH)
    for d in range(1, 4):
        pl.semaphore_signal(barrier, inc=1, device_id=peer_y(d), device_id_type=MESH)
    pl.semaphore_wait(barrier, 17)

    sent = []

    def exchange(phase, count, peer, src, dst):
        here = []
        for d in range(1, count):
            copy = pltpu.make_async_remote_copy(
                src_ref=src(d), dst_ref=dst(d),
                send_sem=send.at[phase, d], recv_sem=recv.at[phase, d],
                device_id=peer(d), device_id_type=MESH,
            )
            copy.start()
            here.append(copy)
        sent.extend(here)
        return here

    def arrive(copies):
        for copy in copies:
            copy.wait_recv()

    copies = exchange(0, 8, peer_z, lambda d: rows.at[lax.rem(z + d, 8)], lambda d: buf1.at[d - 1])
    vpad[:, 384:512] = jnp.zeros((vpad.shape[0], 128), vpad.dtype)
    vpad[:, : vocab.shape[1]] = vocab[...]
    arrive(copies)
    total = rows[z].astype(jnp.float32)
    for d in range(7):
        total = total + buf1[d].astype(jnp.float32)
    acc1[...] = total.astype(jnp.bfloat16)
    copies = exchange(1, 8, peer_p, lambda d: acc1, lambda d: buf2.at[d - 1])
    arrive(copies)
    for d in range(7):
        total = total + buf2[d].astype(jnp.float32)
    chunk[...] = total.astype(jnp.bfloat16)
    copies = exchange(2, 8, peer_z, lambda d: chunk, lambda d: full.at[z])
    full[z] = chunk[...]
    arrive_from = [
        pltpu.make_async_remote_copy(
            src_ref=chunk, dst_ref=full.at[lax.rem(z + 8 - d, 8)],
            send_sem=send.at[2, d], recv_sem=recv.at[2, d],
            device_id=peer_z(d), device_id_type=MESH,
        )
        for d in range(1, 8)
    ]
    arrive(arrive_from)
    wide = full[...].astype(jnp.float32).reshape(REQS, rows.shape[2])
    squares = jnp.sum(wide * wide, axis=1, keepdims=True)
    scaled = wide * gain[...]
    high = scaled.astype(jnp.bfloat16)
    low = (scaled - high.astype(jnp.float32)).astype(jnp.bfloat16)
    logits = jnp.dot(high, vpad[...], preferred_element_type=jnp.float32) + jnp.dot(
        low, vpad[...], preferred_element_type=jnp.float32
    )
    part[...] = logits.astype(jnp.bfloat16).reshape(4, 32, 512)
    sq[...] = jnp.broadcast_to(squares, (REQS, 128)).reshape(4, 32, 128)
    copies = exchange(3, 4, peer_y, lambda d: part.at[lax.rem(y + d, 4)], lambda d: partr.at[d - 1])
    more = exchange(4, 4, peer_y, lambda d: sq.at[lax.rem(y + d, 4)], lambda d: sqr.at[d - 1])
    arrive(copies)
    arrive(more)
    summed = part[y].astype(jnp.float32)
    square = sq[y]
    for d in range(3):
        summed = summed + partr[d].astype(jnp.float32)
        square = square + sqr[d]
    column = lax.broadcasted_iota(jnp.int32, (32, 512), 1)
    best = jnp.max(jnp.where(column < vocab.shape[1], summed, -jnp.inf), axis=1, keepdims=True)
    norm = jnp.sqrt(square / D + 1e-05)
    best = jnp.broadcast_to(best, (32, 128)) / norm
    fin[y, 0] = jnp.transpose(norm)[0:8, :]
    mine[0] = jnp.transpose(best)[0:8, :]
    copies = exchange(5, 8, peer_p, lambda d: mine.at[0], lambda d: buf5.at[d - 1])
    arrive(copies)
    top = mine[0]
    for d in range(7):
        top = jnp.maximum(top, buf5[d])
    mine[1] = top
    copies = exchange(6, 8, peer_z, lambda d: mine.at[1], lambda d: buf6.at[d - 1])
    arrive(copies)
    for d in range(7):
        top = jnp.maximum(top, buf6[d])
    fin[y, 1] = top
    exchange(7, 4, peer_y, lambda d: fin.at[y], lambda d: fin.at[y])
    arrive(
        [
            pltpu.make_async_remote_copy(
                src_ref=fin.at[y], dst_ref=fin.at[lax.rem(y + 4 - d, 4)],
                send_sem=send.at[7, d], recv_sem=recv.at[7, d],
                device_id=peer_y(d), device_id_type=MESH,
            )
            for d in range(1, 4)
        ]
    )
    norm_out[...] = fin[:, 0]
    top_out[...] = fin[:, 1]
    for copy in sent:
        copy.wait_send()


def tail(local_rows, final_gain, w_vocab):
    wide = local_rows.shape[1]
    rows = local_rows.reshape(8, 16, wide)
    bf, f32 = jnp.bfloat16, jnp.float32
    vm = pl.BlockSpec(memory_space=pltpu.VMEM)
    norm, top = pl.pallas_call(
        tail_kernel,
        name="tail",
        out_shape=(jax.ShapeDtypeStruct((4, 8, 32), f32), jax.ShapeDtypeStruct((4, 8, 32), f32)),
        in_specs=[vm] * 3,
        out_specs=[vm] * 2,
        scratch_shapes=[
            pltpu.VMEM((wide, 512), bf),
            pltpu.VMEM((7, 16, wide), bf),
            pltpu.VMEM((16, wide), bf),
            pltpu.VMEM((7, 16, wide), bf),
            pltpu.VMEM((16, wide), bf),
            pltpu.VMEM((8, 16, wide), bf),
            pltpu.VMEM((4, 32, 512), bf),
            pltpu.VMEM((4, 32, 128), f32),
            pltpu.VMEM((3, 32, 512), bf),
            pltpu.VMEM((3, 32, 128), f32),
            pltpu.VMEM((2, 8, 32), f32),
            pltpu.VMEM((7, 8, 32), f32),
            pltpu.VMEM((7, 8, 32), f32),
            pltpu.VMEM((4, 2, 8, 32), f32),
            pltpu.SemaphoreType.DMA((8, 8)),
            pltpu.SemaphoreType.DMA((8, 8)),
        ],
        compiler_params=pltpu.CompilerParams(collective_id=7, has_side_effects=True),
    )(rows, final_gain.reshape(1, wide), w_vocab)
    return norm[:, 0, :].reshape(REQS), top[:, 0, :].reshape(REQS)


def from_behind(array, axis, by):
    devices = lax.axis_size(axis)
    pairs = [(i, i + by) for i in range(devices) if 0 <= i + by < devices]
    return lax.ppermute(array, axis, pairs)


def rotate(field, positions, head_dim):
    middle = head_dim // 2
    inverse = 10000.0 ** (-(jnp.arange(middle, dtype=jnp.float32) * 2.0 / head_dim))
    angles = positions.astype(jnp.float32)[:, None] * inverse[None, :]
    cosine = jnp.cos(angles)[:, None, :]
    sine = jnp.sin(angles)[:, None, :]
    first = field[..., :middle]
    second = field[..., middle:]
    return jnp.concatenate(
        [first * cosine - second * sine, second * cosine + first * sine], axis=-1
    )


def attend(state, block, key_marks, distance, queries, query_marks):
    largest, total, accum = state
    rows = queries.shape[0]
    heads = queries.shape[1]
    head_dim = queries.shape[2]
    paired = block.reshape(block.shape[0], heads, 2 * head_dim)
    keys = paired[..., :head_dim]
    values = paired[..., head_dim:]
    scores = jnp.einsum(
        "qhd,khd->hqk", queries, keys, preferred_element_type=jnp.float32
    ) * head_dim ** (-0.5)
    query_index = jnp.arange(rows, dtype=jnp.int32)[:, None]
    key_index = jnp.arange(block.shape[0], dtype=jnp.int32)[None, :]
    allowed = (
        (query_marks[:, None] == key_marks[None, :])
        & (query_marks[:, None] > 0)
        & (distance * rows + query_index - key_index >= 0)
    )
    masked = jnp.where(allowed[None], scores, NEG)
    newest = jnp.maximum(largest, jnp.max(masked, axis=-1))
    weights = jnp.where(allowed[None], jnp.exp(masked - newest[..., None]), 0.0)
    factor = jnp.exp(largest - newest)
    total = total * factor + jnp.sum(weights, axis=-1)
    accum = accum * factor[..., None] + jnp.einsum(
        "hqk,khd->hqd", weights.astype(jnp.bfloat16), values, preferred_element_type=jnp.float32
    )
    return (newest, total, accum)


def shards(
    tokens,
    norm_gain,
    w_query,
    w_key,
    w_value,
    w_out,
    final_gain,
    w_vocab,
    segment_ids,
    prompt_lengths,
    request_slots,
):
    rows = tokens.shape[0]
    heads = w_query.shape[1] // HD
    seq_index = lax.axis_index("seq")
    whole = lax.all_gather(tokens, "tp", axis=1, tiled=True)
    wide = whole.astype(jnp.float32)
    normed = (
        wide * lax.rsqrt(jnp.mean(wide * wide, axis=-1, keepdims=True) + 1e-05) * norm_gain
    ).astype(jnp.bfloat16)
    starts = jnp.cumsum(prompt_lengths) - prompt_lengths
    matches = segment_ids[:, None] == jnp.arange(prompt_lengths.shape[0], dtype=jnp.int32)[None, :]
    first_slot = jnp.sum(jnp.where(matches, starts[None, :], 0), axis=1)
    slots = seq_index * rows + jnp.arange(rows, dtype=jnp.int32)
    positions = jnp.where(segment_ids >= 0, slots - first_slot, 0)
    query = jnp.dot(normed, w_query, preferred_element_type=jnp.float32).reshape(rows, heads, HD)
    key = jnp.dot(normed, w_key, preferred_element_type=jnp.float32).reshape(rows, heads, HD)
    value = jnp.dot(normed, w_value, preferred_element_type=jnp.float32).reshape(rows, heads, HD)
    rot_query = rotate(query, positions, HD).astype(jnp.bfloat16)
    rot_key = rotate(key, positions, HD).astype(jnp.bfloat16)
    paired = jnp.concatenate([rot_key, value.astype(jnp.bfloat16)], axis=-1)
    kv_cache = jnp.transpose(paired, (1, 0, 2))
    own_block = paired.reshape(rows, heads * 2 * HD)
    marks = jnp.where(segment_ids >= 0, segment_ids + 1, 0)
    span = lax.axis_size("seq") // 4
    attend_here = partial(attend, queries=rot_query, query_marks=marks)

    def visit(state, block, key_marks, distance):
        return attend_here(state, block, key_marks, distance)

    start_state = (
        jnp.full((heads, rows), NEG, jnp.float32),
        jnp.zeros((heads, rows), jnp.float32),
        jnp.zeros((heads, rows, HD), jnp.float32),
    )
    state = attend_here(start_state, own_block, marks, 0)

    def hop(distance, carry):
        current, block, key_marks = carry
        block, key_marks = from_behind((block, key_marks), "seq", 1)
        return (visit(current, block, key_marks, distance), block, key_marks)

    state = lax.fori_loop(1, span + 1, hop, (state, own_block, marks))[0]
    largest, total, accum = state
    attended = (accum / jnp.where(total > 0, total, 1.0)[..., None]).astype(jnp.bfloat16)
    mixed = jnp.transpose(attended, (1, 0, 2)).reshape(rows, heads * HD)
    projected = jnp.dot(mixed, w_out, preferred_element_type=jnp.float32)
    summed = lax.psum_scatter(
        projected.astype(jnp.bfloat16), "tp", scatter_dimension=1, tiled=True
    ).astype(jnp.float32)
    hidden_full = tokens.astype(jnp.float32) + summed
    hidden = hidden_full.astype(jnp.bfloat16)
    picks = (request_slots[:, None] == slots[None, :]).astype(jnp.bfloat16)
    local_rows = jnp.dot(picks, hidden, preferred_element_type=jnp.float32).astype(jnp.bfloat16)
    hidden_norm, top_logit = tail(local_rows, final_gain, w_vocab)
    return (kv_cache, hidden, hidden_norm, top_logit)


def solution(mesh):
    return jax.shard_map(
        shards,
        mesh=mesh,
        in_specs=(
            P("seq", "tp"),
            P(),
            P(None, "tp"),
            P(None, "tp"),
            P(None, "tp"),
            P("tp", None),
            P("tp"),
            P("tp", "seq"),
            P("seq"),
            P(),
            P(),
        ),
        out_specs=(P("tp", "seq", None), P("seq", "tp"), P(), P()),
        check_vma=False,
    )
```

```python
from functools import partial

import jax
import jax.numpy as jnp
import numpy as np
from jax import lax
from jax.experimental import pallas as pl
from jax.experimental.pallas import tpu as pltpu
from jax.sharding import PartitionSpec as P

D = 3072
HD = 96
REQS = 128
MESH = pl.DeviceIdType.MESH


def place():
    s = lax.axis_index("seq")
    return s // 8, s % 8, lax.axis_index("tp")


def tail_kernel(
    rows, gain, vocab, norm_out, top_out,
    vpad, buf1, acc1, buf2, chunk, full, part, sq, partr, sqr, mine, buf5, buf6, fin,
    send, recv,
):
    z, p, y = place()

    def peer_z(d):
        return (lax.rem(z + d, 8) * 8 + p, y)

    def peer_p(d):
        return (z * 8 + lax.rem(p + d, 8), y)

    def peer_y(d):
        return (z * 8 + p, lax.rem(y + d, 4))

    barrier = pltpu.get_barrier_semaphore()
    for d in range(1, 8):
        pl.semaphore_signal(barrier, inc=1, device_id=peer_z(d), device_id_type=MESH)
        pl.semaphore_signal(barrier, inc=1, device_id=peer_p(d), device_id_type=MESH)
    for d in range(1, 4):
        pl.semaphore_signal(barrier, inc=1, device_id=peer_y(d), device_id_type=MESH)
    pl.semaphore_wait(barrier, 17)

    sent = []

    def exchange(phase, count, peer, src, dst):
        here = []
        for d in range(1, count):
            copy = pltpu.make_async_remote_copy(
                src_ref=src(d), dst_ref=dst(d),
                send_sem=send.at[phase, d], recv_sem=recv.at[phase, d],
                device_id=peer(d), device_id_type=MESH,
            )
            copy.start()
            here.append(copy)
        sent.extend(here)
        return here

    def arrive(copies):
        for copy in copies:
            copy.wait_recv()

    copies = exchange(0, 8, peer_z, lambda d: rows.at[lax.rem(z + d, 8)], lambda d: buf1.at[d - 1])
    vpad[:, 384:512] = jnp.zeros((vpad.shape[0], 128), vpad.dtype)
    vpad[:, : vocab.shape[1]] = vocab[...]
    arrive(copies)
    total = rows[z].astype(jnp.float32)
    for d in range(7):
        total = total + buf1[d].astype(jnp.float32)
    acc1[...] = total.astype(jnp.bfloat16)
    copies = exchange(1, 8, peer_p, lambda d: acc1, lambda d: buf2.at[d - 1])
    arrive(copies)
    for d in range(7):
        total = total + buf2[d].astype(jnp.float32)
    chunk[...] = total.astype(jnp.bfloat16)
    copies = exchange(2, 8, peer_z, lambda d: chunk, lambda d: full.at[z])
    full[z] = chunk[...]
    arrive_from = [
        pltpu.make_async_remote_copy(
            src_ref=chunk, dst_ref=full.at[lax.rem(z + 8 - d, 8)],
            send_sem=send.at[2, d], recv_sem=recv.at[2, d],
            device_id=peer_z(d), device_id_type=MESH,
        )
        for d in range(1, 8)
    ]
    arrive(arrive_from)
    wide = full[...].astype(jnp.float32).reshape(REQS, rows.shape[2])
    squares = jnp.sum(wide * wide, axis=1, keepdims=True)
    scaled = wide * gain[...]
    high = scaled.astype(jnp.bfloat16)
    low = (scaled - high.astype(jnp.float32)).astype(jnp.bfloat16)
    logits = jnp.dot(high, vpad[...], preferred_element_type=jnp.float32) + jnp.dot(
        low, vpad[...], preferred_element_type=jnp.float32
    )
    part[...] = logits.astype(jnp.bfloat16).reshape(4, 32, 512)
    sq[...] = jnp.broadcast_to(squares, (REQS, 128)).reshape(4, 32, 128)
    copies = exchange(3, 4, peer_y, lambda d: part.at[lax.rem(y + d, 4)], lambda d: partr.at[d - 1])
    more = exchange(4, 4, peer_y, lambda d: sq.at[lax.rem(y + d, 4)], lambda d: sqr.at[d - 1])
    arrive(copies)
    arrive(more)
    summed = part[y].astype(jnp.float32)
    square = sq[y]
    for d in range(3):
        summed = summed + partr[d].astype(jnp.float32)
        square = square + sqr[d]
    column = lax.broadcasted_iota(jnp.int32, (32, 512), 1)
    best = jnp.max(jnp.where(column < vocab.shape[1], summed, -jnp.inf), axis=1, keepdims=True)
    norm = jnp.sqrt(square / D + 1e-05)
    best = jnp.broadcast_to(best, (32, 128)) / norm
    fin[y, 0] = jnp.transpose(norm)[0:8, :]
    mine[0] = jnp.transpose(best)[0:8, :]
    copies = exchange(5, 8, peer_p, lambda d: mine.at[0], lambda d: buf5.at[d - 1])
    arrive(copies)
    top = mine[0]
    for d in range(7):
        top = jnp.maximum(top, buf5[d])
    mine[1] = top
    copies = exchange(6, 8, peer_z, lambda d: mine.at[1], lambda d: buf6.at[d - 1])
    arrive(copies)
    for d in range(7):
        top = jnp.maximum(top, buf6[d])
    fin[y, 1] = top
    exchange(7, 4, peer_y, lambda d: fin.at[y], lambda d: fin.at[y])
    arrive(
        [
            pltpu.make_async_remote_copy(
                src_ref=fin.at[y], dst_ref=fin.at[lax.rem(y + 4 - d, 4)],
                send_sem=send.at[7, d], recv_sem=recv.at[7, d],
                device_id=peer_y(d), device_id_type=MESH,
            )
            for d in range(1, 4)
        ]
    )
    norm_out[...] = fin[:, 0]
    top_out[...] = fin[:, 1]
    for copy in sent:
        copy.wait_send()


def tail(rows, final_gain, w_vocab):
    wide = rows.shape[2]
    bf, f32 = jnp.bfloat16, jnp.float32
    vm = pl.BlockSpec(memory_space=pltpu.VMEM)
    norm, top = pl.pallas_call(
        tail_kernel,
        name="tail",
        out_shape=(jax.ShapeDtypeStruct((4, 8, 32), f32), jax.ShapeDtypeStruct((4, 8, 32), f32)),
        in_specs=[vm] * 3,
        out_specs=[vm] * 2,
        scratch_shapes=[
            pltpu.VMEM((wide, 512), bf),
            pltpu.VMEM((7, 16, wide), bf),
            pltpu.VMEM((16, wide), bf),
            pltpu.VMEM((7, 16, wide), bf),
            pltpu.VMEM((16, wide), bf),
            pltpu.VMEM((8, 16, wide), bf),
            pltpu.VMEM((4, 32, 512), bf),
            pltpu.VMEM((4, 32, 128), f32),
            pltpu.VMEM((3, 32, 512), bf),
            pltpu.VMEM((3, 32, 128), f32),
            pltpu.VMEM((2, 8, 32), f32),
            pltpu.VMEM((7, 8, 32), f32),
            pltpu.VMEM((7, 8, 32), f32),
            pltpu.VMEM((4, 2, 8, 32), f32),
            pltpu.SemaphoreType.DMA((8, 8)),
            pltpu.SemaphoreType.DMA((8, 8)),
        ],
        compiler_params=pltpu.CompilerParams(collective_id=7, has_side_effects=True),
    )(rows, final_gain.reshape(1, wide), w_vocab)
    return norm[:, 0, :].reshape(REQS), top[:, 0, :].reshape(REQS)


NEG = -1e30
SCALE = HD ** (-0.5) * 1.4426950408889634
INVERSE = 10000.0 ** (-(np.arange(HD // 2, dtype=np.float32) * np.float32(2.0) / np.float32(HD)))


def starts_of(lengths):
    starts, total = [], jnp.int32(0)
    for p in range(8):
        starts.append(total)
        total = total + lengths[p]
    return starts, total


def first_of(slots, starts):
    first = jnp.zeros_like(slots)
    for start in starts[1:]:
        first = jnp.where(slots >= start, start, first)
    return first


def remote(src, dst, send, recv, k, device):
    return pltpu.make_async_remote_copy(
        src_ref=src, dst_ref=dst, send_sem=send.at[k], recv_sem=recv.at[k],
        device_id=device, device_id_type=MESH,
    )


def greet(devices):
    barrier = pltpu.get_barrier_semaphore()
    for device in devices:
        pl.semaphore_signal(barrier, inc=1, device_id=device, device_id_type=MESH)
    pl.semaphore_wait(barrier, len(devices))


def project_kernel(
    lengths, tokens, gain, inverse, wq, wk, wv, out,
    x, normed, wq_v, wk_v, wv_v, cosine, sine, local, send, recv,
):
    s, y = lax.axis_index("seq"), lax.axis_index("tp")
    right, left = (s, lax.rem(y + 1, 4)), (s, lax.rem(y + 3, 4))
    before, after = lax.rem(y + 3, 4), lax.rem(y + 1, 4)
    greet([right, left])

    def rows(c):
        return pl.ds(c * 128, 128)

    def to_right(c):
        return remote(tokens.at[rows(c)], x.at[y, rows(c)], send, recv, c, right)

    def to_left(c):
        return remote(tokens.at[rows(c)], x.at[y, rows(c)], send, recv, 4 + c, left)

    def pass_on(c):
        if c % 2 == 0:
            return remote(x.at[before, rows(c)], x.at[before, rows(c)], send, recv, 8 + c, right)
        return remote(x.at[after, rows(c)], x.at[after, rows(c)], send, recv, 8 + c, left)

    def came(k, c, source):
        return remote(tokens.at[rows(c)], x.at[source, rows(c)], send, recv, k, right)

    sent = []

    def go(copy):
        copy.start()
        sent.append(copy)

    for c in (0, 1):
        go(to_right(c))
        go(to_left(c))
    weights = [
        pltpu.make_async_copy(a, b, local.at[i])
        for i, (a, b) in enumerate(((wk, wk_v), (wv, wv_v), (wq, wq_v)))
    ]
    for copy in weights:
        copy.start()
    x[y] = tokens[...]
    starts, total = starts_of(lengths)
    slots = s * 512 + lax.broadcasted_iota(jnp.int32, (1, 512), 1)
    positions = jnp.where(slots < total, slots - first_of(slots, starts), 0)
    angles = inverse[...] * positions.astype(jnp.float32)
    cosine[...] = jnp.cos(angles)
    sine[...] = jnp.sin(angles)

    def project(half):
        span = slice(half * 256, half * 256 + 256)
        squares = jnp.zeros((256, 1), jnp.float32)
        for f in range(4):
            wide = x[f, span].astype(jnp.float32)
            squares = squares + jnp.sum(wide * wide, axis=1, keepdims=True)
        inverse_norm = lax.rsqrt(squares / D + 1e-05)
        for f in range(4):
            columns = slice(f * 768, f * 768 + 768)
            wide = x[f, span].astype(jnp.float32)
            normed[:, columns] = (wide * inverse_norm * gain[:, columns]).astype(jnp.bfloat16)
        cos, sin = cosine[:, span], sine[:, span]

        def dot(weight):
            return jnp.transpose(
                jnp.dot(normed[...], weight[...], preferred_element_type=jnp.float32)
            )

        def rotated(field, base, scale):
            for h in range(4):
                first = field[h * 96 : h * 96 + 48]
                second = field[h * 96 + 48 : h * 96 + 96]
                a = first * cos - second * sin
                b = second * cos + first * sin
                if scale is not None:
                    a, b = a * scale, b * scale
                out[h, base : base + 48, span] = a.astype(jnp.bfloat16)
                out[h, base + 48 : base + 96, span] = b.astype(jnp.bfloat16)

        rotated(dot(wk_v), 0, None)
        value = dot(wv_v)
        for h in range(4):
            out[h, 96:192, span] = value[h * 96 : h * 96 + 96].astype(jnp.bfloat16)
        rotated(dot(wq_v), 192, SCALE)

    for half in (0, 1):
        even, odd = 2 * half, 2 * half + 1
        came(even, even, before).wait_recv()
        go(pass_on(even))
        came(4 + odd, odd, after).wait_recv()
        go(pass_on(odd))
        if half == 0:
            for c in (2, 3):
                go(to_right(c))
                go(to_left(c))
        came(odd, odd, before).wait_recv()
        came(4 + even, even, after).wait_recv()
        came(8 + even, even, lax.rem(y + 2, 4)).wait_recv()
        came(8 + odd, odd, lax.rem(y + 2, 4)).wait_recv()
        if half == 0:
            for copy in weights:
                copy.wait()
        project(half)
    for copy in sent:
        copy.wait_send()


VM = pl.BlockSpec(memory_space=pltpu.VMEM)
ANY = pl.BlockSpec(memory_space=pl.ANY)
SM = pl.BlockSpec(memory_space=pltpu.SMEM)


def project(tokens, norm_gain, w_query, w_key, w_value, prompt_lengths):
    bf, f32 = jnp.bfloat16, jnp.float32
    return pl.pallas_call(
        project_kernel,
        name="project",
        out_shape=jax.ShapeDtypeStruct((4, 288, 512), bf),
        in_specs=[SM, VM, VM, VM, ANY, ANY, ANY],
        out_specs=VM,
        scratch_shapes=[
            pltpu.VMEM((4, 512, 768), bf),
            pltpu.VMEM((256, D), bf),
            pltpu.VMEM((D, 384), bf),
            pltpu.VMEM((D, 384), bf),
            pltpu.VMEM((D, 384), bf),
            pltpu.VMEM((48, 512), f32),
            pltpu.VMEM((48, 512), f32),
            pltpu.SemaphoreType.DMA((3,)),
            pltpu.SemaphoreType.DMA((12,)),
            pltpu.SemaphoreType.DMA((12,)),
        ],
        compiler_params=pltpu.CompilerParams(
            collective_id=1, has_side_effects=True, vmem_limit_bytes=48 << 20
        ),
    )(prompt_lengths, tokens, norm_gain.reshape(1, D), jnp.asarray(INVERSE).reshape(48, 1),
      w_query, w_key, w_value)


def spread_kernel(qkv, wout, own, sib, q, wo, stage_x, stage_y, send, recv):
    s, y = lax.axis_index("seq"), lax.axis_index("tp")
    z, x, c = s // 8, lax.rem(s, 8) // 2, lax.rem(s, 2)
    step = 1 + 2 * c

    def at_x(d):
        return (z * 8 + lax.rem(x + d, 4) * 2 + c, y)

    def at_y(d):
        return (s, lax.rem(y + d, 4))

    sibling = (z * 8 + x * 2 + (1 - c), y)
    greet([at_x(1), at_x(3), sibling, at_y(1), at_y(3)])
    half = pl.ds(pl.multiple_of(c * 192, 192), 192)

    def columns(d):
        return pl.ds(pl.multiple_of(lax.rem(y + d, 4) * 768, 768), 768)

    sent = []

    def go(*args):
        copy = remote(*args)
        copy.start()
        sent.append(copy)

    def kv(d):
        return qkv.at[lax.rem(x + d, 4), pl.ds(0, 192)]

    def qs(d):
        return qkv.at[lax.rem(x + d, 4), pl.ds(192, 96)]

    go(qkv.at[lax.rem(x + 2, 4)], stage_x, send, recv, 0, at_x(step))
    go(wout.at[half, columns(2)], stage_y, send, recv, 11, at_y(step))
    go(kv(1), own.at[x], send, recv, 1, at_x(1))
    go(kv(3), own.at[x], send, recv, 3, at_x(3))
    go(wout.at[half, columns(1)], wo.at[y, half], send, recv, 12, at_y(1))
    go(wout.at[half, columns(3)], wo.at[y, half], send, recv, 13, at_y(3))
    go(qs(1), q.at[x], send, recv, 2, at_x(1))
    go(qs(3), q.at[x], send, recv, 4, at_x(3))
    go(kv(0), sib.at[x], send, recv, 7, sibling)
    own[x] = qkv[x, 0:192]
    q[x] = qkv[x, 192:288]
    wo[y] = wout[:, columns(0)]

    def came(dst, k):
        remote(dst, dst, send, recv, k, sibling).wait_recv()

    came(stage_x, 0)
    origin = lax.rem(x + 4 - step, 4)
    go(stage_x.at[pl.ds(0, 192)], own.at[origin], send, recv, 5, at_x(step))
    go(stage_x.at[pl.ds(192, 96)], q.at[origin], send, recv, 6, at_x(step))
    came(stage_y, 11)
    go(stage_y, wo.at[lax.rem(y + 4 - step, 4), half], send, recv, 14, at_y(step))
    for k, d in ((1, 3), (3, 1), (5, 2)):
        source = lax.rem(x + d, 4)
        came(own.at[source], k)
        go(own.at[source], sib.at[source], send, recv, 7 + d, sibling)
    for k, d in ((12, 3), (13, 1), (14, 2)):
        source = lax.rem(y + d, 4)
        came(wo.at[source, half], k)
        go(wo.at[source, half], wo.at[source, half], send, recv, 14 + d, sibling)
    for k, d in ((2, 3), (4, 1), (6, 2)):
        came(q.at[lax.rem(x + d, 4)], k)
    for d in range(4):
        came(sib.at[lax.rem(x + d, 4)], 7 + d)
    other = pl.ds(pl.multiple_of((1 - c) * 192, 192), 192)
    for d in range(1, 4):
        came(wo.at[lax.rem(y + d, 4), other], 14 + d)
    for copy in sent:
        copy.wait_send()


def spread(qkv, w_out):
    bf = jnp.bfloat16
    return pl.pallas_call(
        spread_kernel,
        name="spread",
        out_shape=(
            jax.ShapeDtypeStruct((4, 192, 512), bf),
            jax.ShapeDtypeStruct((4, 192, 512), bf),
            jax.ShapeDtypeStruct((4, 96, 512), bf),
            jax.ShapeDtypeStruct((4, 384, 768), bf),
        ),
        in_specs=[VM, VM],
        out_specs=[VM] * 4,
        scratch_shapes=[
            pltpu.VMEM((288, 512), bf),
            pltpu.VMEM((192, 768), bf),
            pltpu.SemaphoreType.DMA((18,)),
            pltpu.SemaphoreType.DMA((18,)),
        ],
        compiler_params=pltpu.CompilerParams(
            collective_id=2, has_side_effects=True, vmem_limit_bytes=32 << 20
        ),
    )(qkv, w_out)


def attend_kernel(hop, last, *refs):
    if hop == 0:
        lengths, q, own, sib, *refs = refs
    else:
        lengths, q, own, sib, acc_in, m_in, *refs = refs
    if last:
        out, keys, values, query, acc, largest = refs
    else:
        acc_out, m_out, keys, values, query, acc, largest = refs
    s = lax.axis_index("seq")
    z, c = s // 8, lax.rem(s, 2)
    starts, total = starts_of(lengths)
    base = (z - hop) * 4096
    filler = jnp.where(lax.broadcasted_iota(jnp.int32, (32, 512), 0) == 0, 1.0, 0.0)
    for b in range(4):
        for ref, k in ((own, 2 * b + c), (sib, 2 * b + 1 - c)):
            keys[k, 0:96] = ref[b, 0:96]
            keys[k, 96:128] = jnp.zeros((32, 512), jnp.bfloat16)
            values[k, 0:96] = ref[b, 96:192]
            values[k, 96:128] = filler.astype(jnp.bfloat16)

    def query_block(b, _):
        begin = (z * 8 + 2 * b + c) * 512
        wide = jnp.concatenate(
            [q[b].astype(jnp.float32), jnp.zeros((32, 512), jnp.float32)], axis=0
        )
        query[...] = jnp.transpose(wide).astype(jnp.bfloat16)
        if hop == 0:
            acc[...] = jnp.zeros_like(acc)
            largest[...] = jnp.full_like(largest, NEG)
        else:
            acc[...] = acc_in[b]
            largest[...] = m_in[b]
        slots = begin + lax.broadcasted_iota(jnp.int32, (512, 1), 0)
        firsts = first_of(slots, starts)

        def visit(k, masked):
            scores = jnp.dot(query[...], keys[k], preferred_element_type=jnp.float32)
            if masked:
                at = base + k * 512 + lax.broadcasted_iota(jnp.int32, (1, 512), 1)
                scores = jnp.where((at >= firsts) & (at <= slots), scores, NEG)
            old = largest[...]
            new = jnp.maximum(old, jnp.max(scores, axis=1, keepdims=True))
            weights = jnp.exp2(scores - new[:, 0:1]).astype(jnp.bfloat16)
            acc[...] = acc[...] * jnp.exp2(old - new) + lax.dot_general(
                weights, values[k], (((1,), (1,)), ((), ())), preferred_element_type=jnp.float32
            )
            largest[...] = new

        end = 8
        if hop == 0:
            end = 2 * b + c
            visit(end, True)
        low = first_of(begin, starts)
        high = first_of(jnp.minimum(begin + 511, total - 1), starts)
        start = jnp.clip((low - base) // 512, 0, end)
        middle = jnp.clip((high - base + 511) // 512, start, end)

        @pl.loop(start, middle)
        def _(k):
            visit(k, True)

        @pl.loop(middle, end)
        def _(k):
            visit(k, False)

        if last:
            result = jnp.where(slots < total, acc[...] / acc[:, 96:97], 0.0)
            out[b] = jnp.transpose(result)[0:96].astype(jnp.bfloat16)
        else:
            acc_out[b] = acc[...]
            m_out[b] = largest[...]
        return 0

    lax.fori_loop(0, 4, query_block, 0)


def attend(hop, last, prompt_lengths, q, own, sib, *state):
    bf, f32 = jnp.bfloat16, jnp.float32
    if last:
        out_shape = jax.ShapeDtypeStruct((4, 96, 512), bf)
        out_specs = VM
    else:
        out_shape = (jax.ShapeDtypeStruct((4, 512, 128), f32),) * 2
        out_specs = [VM] * 2
    pairs = 8 if hop else 5
    return pl.pallas_call(
        partial(attend_kernel, hop, last),
        name=f"attend{hop}",
        out_shape=out_shape,
        in_specs=[SM] + [VM] * (3 + len(state)),
        out_specs=out_specs,
        scratch_shapes=[
            pltpu.VMEM((8, 128, 512), bf),
            pltpu.VMEM((8, 128, 512), bf),
            pltpu.VMEM((512, 128), bf),
            pltpu.VMEM((512, 128), f32),
            pltpu.VMEM((512, 128), f32),
        ],
        compiler_params=pltpu.CompilerParams(vmem_limit_bytes=40 << 20),
        cost_estimate=pl.CostEstimate(
            flops=4 * pairs * 512 * 512 * 512, bytes_accessed=4 << 20,
            transcendentals=4 * pairs * 512 * 512,
        ),
    )(prompt_lengths, q, own, sib, *state)


def finish_kernel(ot, wo, tokens, picks_at, hidden, rows, att, total, send, recv):
    s, y = lax.axis_index("seq"), lax.axis_index("tp")
    z, x, c = s // 8, lax.rem(s, 8) // 2, lax.rem(s, 2)

    def at_x(d):
        return (z * 8 + lax.rem(x + d, 4) * 2 + c, y)

    right, left = (s, lax.rem(y + 1, 4)), (s, lax.rem(y + 3, 4))
    before, after = lax.rem(y + 3, 4), lax.rem(y + 1, 4)
    greet([at_x(1), at_x(2), at_x(3), right, left])
    sent = []

    def go(*args):
        copy = remote(*args)
        copy.start()
        sent.append(copy)

    def came(dst, k):
        remote(dst, dst, send, recv, k, right).wait_recv()

    for d in (2, 1, 3):
        go(ot.at[lax.rem(x + d, 4)], att.at[y, x], send, recv, d, at_x(d))
    att[y, x] = ot[x]
    head = [lax.rem(x + 4 - d, 4) for d in range(4)]
    for d in (0, 1, 3, 2):
        if d == 0:
            piece = ot.at[x]
        else:
            piece = att.at[y, head[d]]
            came(piece, d)
        go(piece, att.at[y, head[d]], send, recv, 4 + d, right)
        go(piece, att.at[y, head[d]], send, recv, 8 + d, left)
    picks = (
        picks_at[...] == s * 512 + lax.broadcasted_iota(jnp.int32, (128, 512), 1)
    ).astype(jnp.bfloat16)

    def term(group):
        return lax.dot_general(
            att[group].reshape(384, 512), wo[group], (((0,), (0,)), ((), ())),
            preferred_element_type=jnp.float32,
        ).astype(jnp.bfloat16).astype(jnp.float32)

    total[...] = tokens[...].astype(jnp.float32) + term(y)
    for d in (0, 1):
        came(att.at[before, head[d]], 4 + d)
        go(att.at[before, head[d]], att.at[before, head[d]], send, recv, 12 + d, right)
    for d in (3, 2):
        came(att.at[after, head[d]], 8 + d)
        go(att.at[after, head[d]], att.at[after, head[d]], send, recv, 12 + d, left)
    for d in (3, 2):
        came(att.at[before, head[d]], 4 + d)
    total[...] += term(before)
    for d in (0, 1):
        came(att.at[after, head[d]], 8 + d)
    total[...] += term(after)
    across = lax.rem(y + 2, 4)
    for d in range(4):
        came(att.at[across, head[d]], 12 + d)
    result = (total[...] + term(across)).astype(jnp.bfloat16)
    hidden[...] = result
    rows[...] = jnp.dot(picks, result, preferred_element_type=jnp.float32).astype(
        jnp.bfloat16
    ).reshape(8, 16, 768)
    for copy in sent:
        copy.wait_send()


def finish(ot, wo, tokens, request_slots):
    bf, f32 = jnp.bfloat16, jnp.float32
    return pl.pallas_call(
        finish_kernel,
        name="finish",
        out_shape=(
            jax.ShapeDtypeStruct((512, 768), bf),
            jax.ShapeDtypeStruct((8, 16, 768), bf),
        ),
        in_specs=[VM] * 4,
        out_specs=[VM] * 2,
        scratch_shapes=[
            pltpu.VMEM((4, 4, 96, 512), bf),
            pltpu.VMEM((512, 768), f32),
            pltpu.SemaphoreType.DMA((16,)),
            pltpu.SemaphoreType.DMA((16,)),
        ],
        compiler_params=pltpu.CompilerParams(
            collective_id=3, has_side_effects=True, vmem_limit_bytes=40 << 20
        ),
    )(ot, wo, tokens, request_slots.reshape(REQS, 1))


def along_z(array):
    return lax.ppermute(array, "seq", [(i, i + 8) for i in range(56)])


def across_chip(array):
    return lax.ppermute(array, "seq", [(i, i ^ 1) for i in range(64)])


def shards(
    tokens, norm_gain, w_query, w_key, w_value, w_out, final_gain, w_vocab,
    segment_ids, prompt_lengths, request_slots,
):
    qkv = project(tokens, norm_gain, w_query, w_key, w_value, prompt_lengths)
    own, sib, q, wo = spread(qkv, w_out)
    kv_cache = jnp.transpose(qkv[:, :192], (0, 2, 1))
    own1 = along_z(own)
    sib1 = across_chip(own1)
    own2 = along_z(own1)
    sib2 = across_chip(own2)
    state = attend(0, False, prompt_lengths, q, own, sib)
    state = attend(1, False, prompt_lengths, q, own1, sib1, *state)
    ot = attend(2, True, prompt_lengths, q, own2, sib2, *state)
    hidden, rows = finish(ot, wo, tokens, request_slots)
    hidden_norm, top_logit = tail(rows, final_gain, w_vocab)
    return (kv_cache, hidden, hidden_norm, top_logit)


def solution(mesh):
    return jax.shard_map(
        shards,
        mesh=mesh,
        in_specs=(
            P("seq", "tp"),
            P(),
            P(None, "tp"),
            P(None, "tp"),
            P(None, "tp"),
            P("tp", None),
            P("tp"),
            P("tp", "seq"),
            P("seq"),
            P(),
            P(),
        ),
        out_specs=(P("tp", "seq", None), P("seq", "tp"), P(), P()),
        check_vma=False,
    )
```

```python
from functools import partial

import jax
import jax.numpy as jnp
import numpy as np
from jax import lax
from jax.experimental import pallas as pl
from jax.experimental.pallas import tpu as pltpu
from jax.sharding import PartitionSpec as P

D = 3072
HD = 96
REQS = 128
MESH = pl.DeviceIdType.MESH


NEG = -1e30
SCALE = HD ** (-0.5) * 1.4426950408889634
INVERSE = 10000.0 ** (-(np.arange(HD // 2, dtype=np.float32) * np.float32(2.0) / np.float32(HD)))


def starts_of(lengths):
    starts, total = [], jnp.int32(0)
    for p in range(8):
        starts.append(total)
        total = total + lengths[p]
    return starts, total


def first_of(slots, starts):
    first = jnp.zeros_like(slots)
    for start in starts[1:]:
        first = jnp.where(slots >= start, start, first)
    return first


def remote(src, dst, send, recv, k, device):
    return pltpu.make_async_remote_copy(
        src_ref=src, dst_ref=dst, send_sem=send.at[k], recv_sem=recv.at[k],
        device_id=device, device_id_type=MESH,
    )


def greet(devices):
    barrier = pltpu.get_barrier_semaphore()
    for device in devices:
        pl.semaphore_signal(barrier, inc=1, device_id=device, device_id_type=MESH)
    pl.semaphore_wait(barrier, len(devices))


def project_kernel(
    lengths_in, tokens, gain_in, inverse_in, wq, wk, wv, out,
    lengths, gain, inverse, x, normed, wq_v, wk_v, wv_v, cosine, sine, local, send, recv,
):
    s, y = lax.axis_index("seq"), lax.axis_index("tp")
    right, left = (s, lax.rem(y + 1, 4)), (s, lax.rem(y + 3, 4))
    before, after = lax.rem(y + 3, 4), lax.rem(y + 1, 4)
    greet([right, left])

    def rows(c):
        return pl.ds(c * 128, 128)

    def to_right(c):
        return remote(tokens.at[rows(c)], x.at[y, rows(c)], send, recv, c, right)

    def to_left(c):
        return remote(tokens.at[rows(c)], x.at[y, rows(c)], send, recv, 4 + c, left)

    def pass_on(c):
        if c % 2 == 0:
            return remote(x.at[before, rows(c)], x.at[before, rows(c)], send, recv, 8 + c, right)
        return remote(x.at[after, rows(c)], x.at[after, rows(c)], send, recv, 8 + c, left)

    def came(k, c, source):
        return remote(tokens.at[rows(c)], x.at[source, rows(c)], send, recv, k, right)

    sent = []

    def go(copy):
        copy.start()
        sent.append(copy)

    for c in (0, 1):
        go(to_right(c))
        go(to_left(c))
    loads = [
        pltpu.make_async_copy(a, b, local.at[i])
        for i, (a, b) in enumerate((
            (lengths_in, lengths), (inverse_in, inverse), (gain_in, gain), (tokens, x.at[y]),
            (wk, wk_v), (wv, wv_v), (wq, wq_v),
        ))
    ]
    for copy in loads:
        copy.start()
    loads[0].wait()
    loads[1].wait()
    starts, total = starts_of(lengths)
    slots = s * 512 + lax.broadcasted_iota(jnp.int32, (1, 512), 1)
    positions = jnp.where(slots < total, slots - first_of(slots, starts), 0)
    angles = inverse[...] * positions.astype(jnp.float32)
    cosine[...] = jnp.cos(angles)
    sine[...] = jnp.sin(angles)

    def project(half):
        span = slice(half * 256, half * 256 + 256)
        squares = jnp.zeros((256, 1), jnp.float32)
        for f in range(4):
            wide = x[f, span].astype(jnp.float32)
            squares = squares + jnp.sum(wide * wide, axis=1, keepdims=True)
        inverse_norm = lax.rsqrt(squares / D + 1e-05)
        for f in range(4):
            columns = slice(f * 768, f * 768 + 768)
            wide = x[f, span].astype(jnp.float32)
            normed[:, columns] = (wide * inverse_norm * gain[:, columns]).astype(jnp.bfloat16)
        cos, sin = cosine[:, span], sine[:, span]

        def dot(weight):
            return jnp.transpose(
                jnp.dot(normed[...], weight[...], preferred_element_type=jnp.float32)
            )

        def rotated(field, base, scale):
            for h in range(4):
                first = field[h * 96 : h * 96 + 48]
                second = field[h * 96 + 48 : h * 96 + 96]
                a = first * cos - second * sin
                b = second * cos + first * sin
                if scale is not None:
                    a, b = a * scale, b * scale
                out[h, base : base + 48, span] = a.astype(jnp.bfloat16)
                out[h, base + 48 : base + 96, span] = b.astype(jnp.bfloat16)

        rotated(dot(wk_v), 0, None)
        value = dot(wv_v)
        for h in range(4):
            out[h, 96:192, span] = value[h * 96 : h * 96 + 96].astype(jnp.bfloat16)
        rotated(dot(wq_v), 192, SCALE)

    for half in (0, 1):
        even, odd = 2 * half, 2 * half + 1
        came(even, even, before).wait_recv()
        go(pass_on(even))
        came(4 + odd, odd, after).wait_recv()
        go(pass_on(odd))
        if half == 0:
            for c in (2, 3):
                go(to_right(c))
                go(to_left(c))
        came(odd, odd, before).wait_recv()
        came(4 + even, even, after).wait_recv()
        came(8 + even, even, lax.rem(y + 2, 4)).wait_recv()
        came(8 + odd, odd, lax.rem(y + 2, 4)).wait_recv()
        if half == 0:
            for copy in loads[2:]:
                copy.wait()
        project(half)
    for copy in sent:
        copy.wait_send()


VM = pl.BlockSpec(memory_space=pltpu.VMEM)
ANY = pl.BlockSpec(memory_space=pl.ANY)
SM = pl.BlockSpec(memory_space=pltpu.SMEM)


def project(tokens, norm_gain, w_query, w_key, w_value, prompt_lengths):
    bf, f32 = jnp.bfloat16, jnp.float32
    return pl.pallas_call(
        project_kernel,
        name="project",
        out_shape=jax.ShapeDtypeStruct((4, 288, 512), bf),
        in_specs=[ANY] * 7,
        out_specs=VM,
        scratch_shapes=[
            pltpu.SMEM((8,), jnp.int32),
            pltpu.VMEM((1, D), f32),
            pltpu.VMEM((48, 1), f32),
            pltpu.VMEM((4, 512, 768), bf),
            pltpu.VMEM((256, D), bf),
            pltpu.VMEM((D, 384), bf),
            pltpu.VMEM((D, 384), bf),
            pltpu.VMEM((D, 384), bf),
            pltpu.VMEM((48, 512), f32),
            pltpu.VMEM((48, 512), f32),
            pltpu.SemaphoreType.DMA((7,)),
            pltpu.SemaphoreType.DMA((12,)),
            pltpu.SemaphoreType.DMA((12,)),
        ],
        compiler_params=pltpu.CompilerParams(
            collective_id=1, has_side_effects=True, vmem_limit_bytes=60 << 20
        ),
    )(prompt_lengths, tokens, norm_gain.reshape(1, D), jnp.asarray(INVERSE).reshape(48, 1),
      w_query, w_key, w_value)


def spread_kernel(
    qkv, wout, own, sib, own1, sib1, q, wo, stage_x, stage_y, local, send, recv
):
    s, y = lax.axis_index("seq"), lax.axis_index("tp")
    z, x, c = s // 8, lax.rem(s, 8) // 2, lax.rem(s, 2)
    step = 1 + 2 * c

    def at_x(d):
        return (z * 8 + lax.rem(x + d, 4) * 2 + c, y)

    def at_y(d):
        return (s, lax.rem(y + d, 4))

    sibling = (z * 8 + x * 2 + (1 - c), y)
    above = (lax.rem(z + 1, 8) * 8 + x * 2 + c, y)
    below = (lax.rem(z + 7, 8) * 8 + x * 2 + c, y)
    greet([at_x(1), at_x(3), sibling, at_y(1), at_y(3), above, below])
    half = pl.ds(pl.multiple_of(c * 192, 192), 192)

    def columns(d):
        return pl.ds(pl.multiple_of(lax.rem(y + d, 4) * 768, 768), 768)

    sent = []

    def go(*args):
        copy = remote(*args)
        copy.start()
        sent.append(copy)

    def kv(d):
        return qkv.at[lax.rem(x + d, 4), pl.ds(0, 192)]

    def qs(d):
        return qkv.at[lax.rem(x + d, 4), pl.ds(192, 96)]

    go(qkv.at[lax.rem(x + 2, 4)], stage_x, send, recv, 0, at_x(step))
    go(wout.at[half, columns(2)], stage_y, send, recv, 11, at_y(step))
    go(kv(1), own.at[x], send, recv, 1, at_x(1))
    go(kv(3), own.at[x], send, recv, 3, at_x(3))
    go(wout.at[half, columns(1)], wo.at[y, half], send, recv, 12, at_y(1))
    go(wout.at[half, columns(3)], wo.at[y, half], send, recv, 13, at_y(3))
    go(qs(1), q.at[x], send, recv, 2, at_x(1))
    go(qs(3), q.at[x], send, recv, 4, at_x(3))
    go(kv(0), own1.at[x], send, recv, 18, above)
    go(kv(0), sib.at[x], send, recv, 7, sibling)
    kept = [
        pltpu.make_async_copy(kv(0), own.at[x], local.at[0]),
        pltpu.make_async_copy(qs(0), q.at[x], local.at[1]),
        pltpu.make_async_copy(wout.at[:, columns(0)], wo.at[y], local.at[2]),
    ]
    for copy in kept:
        copy.start()

    def came(dst, k):
        remote(dst, dst, send, recv, k, sibling).wait_recv()

    came(stage_x, 0)
    origin = lax.rem(x + 4 - step, 4)
    go(stage_x.at[pl.ds(0, 192)], own.at[origin], send, recv, 5, at_x(step))
    go(stage_x.at[pl.ds(192, 96)], q.at[origin], send, recv, 6, at_x(step))
    came(stage_y, 11)
    go(stage_y, wo.at[lax.rem(y + 4 - step, 4), half], send, recv, 14, at_y(step))
    for k, d in ((1, 3), (3, 1), (5, 2)):
        source = lax.rem(x + d, 4)
        came(own.at[source], k)
        go(own.at[source], own1.at[source], send, recv, 18 + d, above)
        go(own.at[source], sib.at[source], send, recv, 7 + d, sibling)
    for k, d in ((12, 3), (13, 1), (14, 2)):
        source = lax.rem(y + d, 4)
        came(wo.at[source, half], k)
        go(wo.at[source, half], wo.at[source, half], send, recv, 14 + d, sibling)
    for k, d in ((2, 3), (4, 1), (6, 2)):
        came(q.at[lax.rem(x + d, 4)], k)
    for d in (0, 3, 1, 2):
        source = lax.rem(x + d, 4)
        came(own1.at[source], 18 + d)
        go(own1.at[source], sib1.at[source], send, recv, 22 + d, sibling)
    for d in range(4):
        came(sib.at[lax.rem(x + d, 4)], 7 + d)
        came(sib1.at[lax.rem(x + d, 4)], 22 + d)
    other = pl.ds(pl.multiple_of((1 - c) * 192, 192), 192)
    for d in range(1, 4):
        came(wo.at[lax.rem(y + d, 4), other], 14 + d)
    for copy in kept:
        copy.wait()
    for copy in sent:
        copy.wait_send()


def spread(qkv, w_out):
    bf = jnp.bfloat16
    return pl.pallas_call(
        spread_kernel,
        name="spread",
        out_shape=(
            *(jax.ShapeDtypeStruct((4, 192, 512), bf),) * 4,
            jax.ShapeDtypeStruct((4, 96, 512), bf),
            jax.ShapeDtypeStruct((4, 384, 768), bf),
        ),
        in_specs=[ANY, ANY],
        out_specs=[VM] * 6,
        scratch_shapes=[
            pltpu.VMEM((288, 512), bf),
            pltpu.VMEM((192, 768), bf),
            pltpu.SemaphoreType.DMA((3,)),
            pltpu.SemaphoreType.DMA((26,)),
            pltpu.SemaphoreType.DMA((26,)),
        ],
        compiler_params=pltpu.CompilerParams(
            collective_id=2, has_side_effects=True, vmem_limit_bytes=32 << 20
        ),
    )(qkv, w_out)


def attend_kernel(planes, resume, *refs):
    lengths, q, *refs = refs
    pairs, refs = refs[: 2 * len(planes)], refs[2 * len(planes) :]
    if resume:
        acc_in, m_in, out, keys, values, query, acc, largest = refs
    else:
        acc_out, m_out, keys, values, query, acc, largest = refs
    s = lax.axis_index("seq")
    z, c = s // 8, lax.rem(s, 2)
    starts, total = starts_of(lengths)
    base = (z - planes[0]) * 4096
    filler = jnp.where(lax.broadcasted_iota(jnp.int32, (32, 512), 0) == 0, 1.0, 0.0)
    for i in range(len(planes)):
        for b in range(4):
            for ref, k in ((pairs[2 * i], 2 * b + c), (pairs[2 * i + 1], 2 * b + 1 - c)):
                keys[8 * i + k, 0:96] = ref[b, 0:96]
                keys[8 * i + k, 96:128] = jnp.zeros((32, 512), jnp.bfloat16)
                values[8 * i + k, 0:96] = ref[b, 96:192]
                values[8 * i + k, 96:128] = filler.astype(jnp.bfloat16)

    def query_block(b, _):
        begin = (z * 8 + 2 * b + c) * 512
        wide = jnp.concatenate(
            [q[b].astype(jnp.float32), jnp.zeros((32, 512), jnp.float32)], axis=0
        )
        query[...] = jnp.transpose(wide).astype(jnp.bfloat16)
        if resume:
            acc[...] = acc_in[b]
            largest[...] = m_in[b]
        else:
            acc[...] = jnp.zeros_like(acc)
            largest[...] = jnp.full_like(largest, NEG)
        slots = begin + lax.broadcasted_iota(jnp.int32, (512, 1), 0)
        firsts = first_of(slots, starts)

        def visit(k, count, masked):
            halves = [slice(0, 256), slice(256, 512)]
            scores = [
                [
                    jnp.dot(query[half], keys[k + i], preferred_element_type=jnp.float32)
                    for i in range(count)
                ]
                for half in halves
            ]
            for half, parts in zip(halves, scores):
                if masked:
                    at = base + k * 512 + lax.broadcasted_iota(jnp.int32, (1, 512), 1)
                    seen = (at >= firsts[half]) & (at <= slots[half])
                    parts = [jnp.where(seen, parts[0], NEG)]
                most = parts[0]
                for part in parts[1:]:
                    most = jnp.maximum(most, part)
                old = largest[half]
                new = jnp.maximum(old, jnp.max(most, axis=1, keepdims=True))
                sums = acc[half] * jnp.exp2(old - new)
                for i, part in enumerate(parts):
                    weights = jnp.exp2(part - new[:, 0:1]).astype(jnp.bfloat16)
                    sums = sums + lax.dot_general(
                        weights, values[k + i], (((1,), (1,)), ((), ())),
                        preferred_element_type=jnp.float32,
                    )
                acc[half] = sums
                largest[half] = new

        end = 8 * len(planes)
        if not resume:
            end = end - 8 + 2 * b + c
            visit(end, 1, True)
        low = first_of(begin, starts)
        high = first_of(jnp.minimum(begin + 511, total - 1), starts)
        start = jnp.clip((low - base) // 512, 0, end)
        middle = jnp.clip((high - base + 511) // 512, start, end)
        twos = (end - middle) // 2

        @pl.loop(start, middle)
        def _(k):
            visit(k, 1, True)

        @pl.loop(0, twos)
        def _(k):
            visit(middle + 2 * k, 2, False)

        @pl.when(middle + 2 * twos < end)
        def _():
            visit(end - 1, 1, False)

        if resume:
            result = jnp.where(slots < total, acc[...] / acc[:, 96:97], 0.0)
            out[b] = jnp.transpose(result)[0:96].astype(jnp.bfloat16)
        else:
            acc_out[b] = acc[...]
            m_out[b] = largest[...]
        return 0

    lax.fori_loop(0, 4, query_block, 0)


def attend(planes, prompt_lengths, q, blocks, state=()):
    bf, f32 = jnp.bfloat16, jnp.float32
    resume = len(state) > 0
    if resume:
        out_shape = jax.ShapeDtypeStruct((4, 96, 512), bf)
        out_specs = VM
    else:
        out_shape = (jax.ShapeDtypeStruct((4, 512, 128), f32),) * 2
        out_specs = [VM] * 2
    steps = 4 if resume else 13
    return pl.pallas_call(
        partial(attend_kernel, planes, resume),
        name="attend_far" if resume else "attend_near",
        out_shape=out_shape,
        in_specs=[SM] + [VM] * (1 + len(blocks) + len(state)),
        out_specs=out_specs,
        scratch_shapes=[
            pltpu.VMEM((8 * len(planes), 128, 512), bf),
            pltpu.VMEM((8 * len(planes), 128, 512), bf),
            pltpu.VMEM((512, 128), bf),
            pltpu.VMEM((512, 128), f32),
            pltpu.VMEM((512, 128), f32),
        ],
        compiler_params=pltpu.CompilerParams(vmem_limit_bytes=24 << 20),
        cost_estimate=pl.CostEstimate(
            flops=4 * steps * 4 * 512 * 512 * 256, bytes_accessed=8 << 20,
            transcendentals=4 * steps * 512 * 512,
        ),
    )(prompt_lengths, q, *blocks, *state)


def finish_kernel(
    ot, wo, tokens, request_slots, gain, vocab, hidden, norm_out, top_out,
    att, total, rows, vpad, buf1, acc1, buf2, chunk, full, part, sq, partr, sqr, mine,
    buf5, buf6, fin, send, recv, tsend, trecv,
):
    s, y = lax.axis_index("seq"), lax.axis_index("tp")
    z, p = s // 8, lax.rem(s, 8)
    x, c = p // 2, lax.rem(p, 2)

    def at_x(d):
        return (z * 8 + lax.rem(x + d, 4) * 2 + c, y)

    def peer_z(d):
        return (lax.rem(z + d, 8) * 8 + p, y)

    def peer_p(d):
        return (z * 8 + lax.rem(p + d, 8), y)

    def peer_y(d):
        return (s, lax.rem(y + d, 4))

    right, left = peer_y(1), peer_y(3)
    before, after = lax.rem(y + 3, 4), lax.rem(y + 1, 4)
    greet(
        [peer_p(d) for d in range(1, 8)]
        + [peer_y(d) for d in range(1, 4)]
        + [peer_z(d) for d in range(1, 8)]
    )
    sent = []

    def go(*args):
        copy = remote(*args)
        copy.start()
        sent.append(copy)

    def came(dst, k):
        remote(dst, dst, send, recv, k, right).wait_recv()

    for d in (2, 1, 3):
        go(ot.at[lax.rem(x + d, 4)], att.at[y, x], send, recv, d, at_x(d))
    att[y, x] = ot[x]
    head = [lax.rem(x + 4 - d, 4) for d in range(4)]
    for d in (0, 1, 3, 2):
        if d == 0:
            piece = ot.at[x]
        else:
            piece = att.at[y, head[d]]
            came(piece, d)
        go(piece, att.at[y, head[d]], send, recv, 4 + d, right)
        go(piece, att.at[y, head[d]], send, recv, 8 + d, left)
    picks = (
        request_slots[...] == s * 512 + lax.broadcasted_iota(jnp.int32, (512, 128), 0)
    ).astype(jnp.bfloat16)
    columns = vocab.shape[0]
    vpad[496:512] = jnp.zeros((16, 768), jnp.bfloat16)
    vpad[0:columns] = vocab[...]

    def term(group):
        return lax.dot_general(
            att[group].reshape(384, 512), wo[group], (((0,), (0,)), ((), ())),
            preferred_element_type=jnp.float32,
        ).astype(jnp.bfloat16).astype(jnp.float32)

    total[...] = tokens[...].astype(jnp.float32) + term(y)
    for d in (0, 1):
        came(att.at[before, head[d]], 4 + d)
        go(att.at[before, head[d]], att.at[before, head[d]], send, recv, 12 + d, right)
    for d in (3, 2):
        came(att.at[after, head[d]], 8 + d)
        go(att.at[after, head[d]], att.at[after, head[d]], send, recv, 12 + d, left)
    for d in (3, 2):
        came(att.at[before, head[d]], 4 + d)
    total[...] += term(before)
    for d in (0, 1):
        came(att.at[after, head[d]], 8 + d)
    total[...] += term(after)
    across = lax.rem(y + 2, 4)
    for d in range(4):
        came(att.at[across, head[d]], 12 + d)
    result = (total[...] + term(across)).astype(jnp.bfloat16)
    hidden[...] = result
    rows[...] = lax.dot_general(
        picks, result, (((0,), (0,)), ((), ())), preferred_element_type=jnp.float32
    ).astype(jnp.bfloat16).reshape(8, 16, 768)

    def exchange(phase, count, peer, src, dst, landed=None):
        arrivals = []
        for d in range(1, count):
            copy = remote(src(d), dst(d), tsend, trecv, (phase, d), peer(d))
            copy.start()
            sent.append(copy)
            where = dst(d) if landed is None else landed(d)
            arrivals.append(remote(src(d), where, tsend, trecv, (phase, d), peer(d)))
        return arrivals

    def arrive(copies):
        for copy in copies:
            copy.wait_recv()

    arrive(exchange(
        0, 8, peer_p, lambda d: rows.at[lax.rem(p + d, 8)], lambda d: buf1.at[d - 1]
    ))
    mix = rows[p].astype(jnp.float32)
    for d in range(7):
        mix = mix + buf1[d].astype(jnp.float32)
    acc1[...] = mix.astype(jnp.bfloat16)
    arrive(exchange(1, 8, peer_z, lambda d: acc1, lambda d: buf2.at[d - 1]))
    for d in range(7):
        mix = mix + buf2[d].astype(jnp.float32)
    chunk[...] = mix.astype(jnp.bfloat16)
    copies = exchange(
        2, 8, peer_p, lambda d: chunk, lambda d: full.at[p],
        lambda d: full.at[lax.rem(p + 8 - d, 8)],
    )
    full[p] = chunk[...]
    arrive(copies)
    wide = full[...].astype(jnp.float32).reshape(REQS, 768)
    squares = jnp.sum(wide * wide, axis=1, keepdims=True)
    scaled = wide * gain[...]
    high = scaled.astype(jnp.bfloat16)
    low = (scaled - high.astype(jnp.float32)).astype(jnp.bfloat16)

    def against_vocab(a):
        return lax.dot_general(
            a, vpad[...], (((1,), (1,)), ((), ())), preferred_element_type=jnp.float32
        )

    part[...] = (against_vocab(high) + against_vocab(low)).astype(jnp.bfloat16).reshape(4, 32, 512)
    sq[...] = jnp.broadcast_to(squares, (REQS, 128)).reshape(4, 32, 128)
    copies = exchange(3, 4, peer_y, lambda d: part.at[lax.rem(y + d, 4)], lambda d: partr.at[d - 1])
    copies += exchange(4, 4, peer_y, lambda d: sq.at[lax.rem(y + d, 4)], lambda d: sqr.at[d - 1])
    arrive(copies)
    summed = part[y].astype(jnp.float32)
    square = sq[y]
    for d in range(3):
        summed = summed + partr[d].astype(jnp.float32)
        square = square + sqr[d]
    column = lax.broadcasted_iota(jnp.int32, (32, 512), 1)
    best = jnp.max(jnp.where(column < columns, summed, -jnp.inf), axis=1, keepdims=True)
    norm = jnp.sqrt(square / D + 1e-05)
    best = jnp.broadcast_to(best, (32, 128)) / norm
    fin[y, 0] = jnp.transpose(norm)[0:8, :]
    mine[0] = jnp.transpose(best)[0:8, :]
    arrive(exchange(5, 8, peer_p, lambda d: mine.at[0], lambda d: buf5.at[d - 1]))
    top = mine[0]
    for d in range(7):
        top = jnp.maximum(top, buf5[d])
    mine[1] = top
    arrive(exchange(6, 8, peer_z, lambda d: mine.at[1], lambda d: buf6.at[d - 1]))
    for d in range(7):
        top = jnp.maximum(top, buf6[d])
    fin[y, 1] = top
    arrive(exchange(
        7, 4, peer_y, lambda d: fin.at[y], lambda d: fin.at[y],
        lambda d: fin.at[lax.rem(y + 4 - d, 4)],
    ))
    norm_out[...] = fin[:, 0]
    top_out[...] = fin[:, 1]
    for copy in sent:
        copy.wait_send()


def finish(ot, wo, tokens, request_slots, final_gain, w_vocab):
    bf, f32 = jnp.bfloat16, jnp.float32
    hidden, norm, top = pl.pallas_call(
        finish_kernel,
        name="finish",
        out_shape=(
            jax.ShapeDtypeStruct((512, 768), bf),
            jax.ShapeDtypeStruct((4, 8, 32), f32),
            jax.ShapeDtypeStruct((4, 8, 32), f32),
        ),
        in_specs=[VM] * 6,
        out_specs=[VM] * 3,
        scratch_shapes=[
            pltpu.VMEM((4, 4, 96, 512), bf),
            pltpu.VMEM((512, 768), f32),
            pltpu.VMEM((8, 16, 768), bf),
            pltpu.VMEM((512, 768), bf),
            pltpu.VMEM((7, 16, 768), bf),
            pltpu.VMEM((16, 768), bf),
            pltpu.VMEM((7, 16, 768), bf),
            pltpu.VMEM((16, 768), bf),
            pltpu.VMEM((8, 16, 768), bf),
            pltpu.VMEM((4, 32, 512), bf),
            pltpu.VMEM((4, 32, 128), f32),
            pltpu.VMEM((3, 32, 512), bf),
            pltpu.VMEM((3, 32, 128), f32),
            pltpu.VMEM((2, 8, 32), f32),
            pltpu.VMEM((7, 8, 32), f32),
            pltpu.VMEM((7, 8, 32), f32),
            pltpu.VMEM((4, 2, 8, 32), f32),
            pltpu.SemaphoreType.DMA((16,)),
            pltpu.SemaphoreType.DMA((16,)),
            pltpu.SemaphoreType.DMA((8, 8)),
            pltpu.SemaphoreType.DMA((8, 8)),
        ],
        compiler_params=pltpu.CompilerParams(
            collective_id=3, has_side_effects=True, vmem_limit_bytes=32 << 20
        ),
    )(ot, wo, tokens, request_slots.reshape(1, REQS), final_gain.reshape(1, 768), w_vocab.T)
    return hidden, norm[:, 0, :].reshape(REQS), top[:, 0, :].reshape(REQS)


def along_z(array):
    return lax.ppermute(array, "seq", [(i, i + 8) for i in range(56)])


def across_chip(array):
    return lax.ppermute(array, "seq", [(i, i ^ 1) for i in range(64)])


def shards(
    tokens, norm_gain, w_query, w_key, w_value, w_out, final_gain, w_vocab,
    segment_ids, prompt_lengths, request_slots,
):
    qkv = project(tokens, norm_gain, w_query, w_key, w_value, prompt_lengths)
    own, sib, own1, sib1, q, wo = spread(qkv, w_out)
    kv_cache = jnp.transpose(qkv[:, :192], (0, 2, 1))
    own2 = along_z(own1)
    state = attend((1, 0), prompt_lengths, q, (own1, sib1, own, sib))
    own2, *state = lax.optimization_barrier((own2, *state))
    sib2 = across_chip(own2)
    ot = attend((2,), prompt_lengths, q, (own2, sib2), state)
    hidden, hidden_norm, top_logit = finish(
        ot, wo, tokens, request_slots, final_gain, w_vocab
    )
    return (kv_cache, hidden, hidden_norm, top_logit)


def solution(mesh):
    return jax.shard_map(
        shards,
        mesh=mesh,
        in_specs=(
            P("seq", "tp"),
            P(),
            P(None, "tp"),
            P(None, "tp"),
            P(None, "tp"),
            P("tp", None),
            P("tp"),
            P("tp", "seq"),
            P("seq"),
            P(),
            P(),
        ),
        out_specs=(P("tp", "seq", None), P("seq", "tp"), P(), P()),
        check_vma=False,
    )
```

```python
from functools import partial

import jax
import jax.numpy as jnp
import numpy as np
from jax import lax
from jax.experimental import pallas as pl
from jax.experimental.pallas import tpu as pltpu
from jax.sharding import PartitionSpec as P

D = 3072
HD = 96
REQS = 128
MESH = pl.DeviceIdType.MESH


NEG = -1e30
SCALE = HD ** (-0.5) * 1.4426950408889634
INVERSE = 10000.0 ** (-(np.arange(HD // 2, dtype=np.float32) * np.float32(2.0) / np.float32(HD)))


def starts_of(lengths):
    starts, total = [], jnp.int32(0)
    for p in range(8):
        starts.append(total)
        total = total + lengths[p]
    return starts, total


def first_of(slots, starts):
    first = jnp.zeros_like(slots)
    for start in starts[1:]:
        first = jnp.where(slots >= start, start, first)
    return first


def remote(src, dst, send, recv, k, device):
    return pltpu.make_async_remote_copy(
        src_ref=src, dst_ref=dst, send_sem=send.at[k], recv_sem=recv.at[k],
        device_id=device, device_id_type=MESH,
    )


def greet(devices):
    barrier = pltpu.get_barrier_semaphore()
    for device in devices:
        pl.semaphore_signal(barrier, inc=1, device_id=device, device_id_type=MESH)
    pl.semaphore_wait(barrier, len(devices))


def project_kernel(
    lengths_in, tokens, gain_in, wq, wk, wv, wout,
    out, own, sib, own1, sib1, q, wo,
    lengths, gain, x, normed, wq_v, wk_v, wv_v, cosine, sine, stage_x, stage_y,
    local, send, recv, hsend, hrecv, wsend, wrecv,
):
    s, y = lax.axis_index("seq"), lax.axis_index("tp")
    z, xi, c = s // 8, lax.rem(s, 8) // 2, lax.rem(s, 2)
    step = 1 + 2 * c

    def at_x(d):
        return (z * 8 + lax.rem(xi + d, 4) * 2 + c, y)

    def at_y(d):
        return (s, lax.rem(y + d, 4))

    right, left = at_y(1), at_y(3)
    before, after = lax.rem(y + 3, 4), lax.rem(y + 1, 4)
    sibling = (z * 8 + xi * 2 + (1 - c), y)
    above = (lax.rem(z + 1, 8) * 8 + xi * 2 + c, y)
    below = (lax.rem(z + 7, 8) * 8 + xi * 2 + c, y)
    greet([right, left, at_x(1), at_x(3), sibling, above, below])

    def rows(c):
        return pl.ds(c * 128, 128)

    def to_right(c):
        return remote(tokens.at[rows(c)], x.at[y, rows(c)], send, recv, c, right)

    def to_left(c):
        return remote(tokens.at[rows(c)], x.at[y, rows(c)], send, recv, 4 + c, left)

    def pass_on(c):
        if c % 2 == 0:
            return remote(x.at[before, rows(c)], x.at[before, rows(c)], send, recv, 8 + c, right)
        return remote(x.at[after, rows(c)], x.at[after, rows(c)], send, recv, 8 + c, left)

    def came(k, c, source):
        return remote(tokens.at[rows(c)], x.at[source, rows(c)], send, recv, k, right)

    sent = []

    def go(copy):
        copy.start()
        sent.append(copy)

    for n in (0, 1):
        go(to_right(n))
        go(to_left(n))
    loads = [
        pltpu.make_async_copy(a, b, local.at[i])
        for i, (a, b) in enumerate((
            (lengths_in, lengths), (gain_in, gain), (tokens, x.at[y]),
            (wk, wk_v), (wv, wv_v), (wq, wq_v),
            (wout.at[:, pl.ds(pl.multiple_of(y * 768, 768), 768)], wo.at[y]),
        ))
    ]
    for copy in loads:
        copy.start()
    loads[0].wait()
    starts, total = starts_of(lengths)
    slots = s * 512 + lax.broadcasted_iota(jnp.int32, (1, 512), 1)
    positions = jnp.where(slots < total, slots - first_of(slots, starts), 0)
    row = lax.broadcasted_iota(jnp.int32, (48, 1), 0)
    inverse = jnp.full((48, 1), float(INVERSE[0]), jnp.float32)
    for i in range(1, 48):
        inverse = jnp.where(row == i, float(INVERSE[i]), inverse)
    angles = inverse * positions.astype(jnp.float32)
    cosine[...] = jnp.cos(angles)
    sine[...] = jnp.sin(angles)

    def project(half):
        span = slice(half * 256, half * 256 + 256)
        squares = jnp.zeros((256, 1), jnp.float32)
        for f in range(4):
            wide = x[f, span].astype(jnp.float32)
            squares = squares + jnp.sum(wide * wide, axis=1, keepdims=True)
        inverse_norm = lax.rsqrt(squares / D + 1e-05)
        for f in range(4):
            columns = slice(f * 768, f * 768 + 768)
            wide = x[f, span].astype(jnp.float32)
            normed[:, columns] = (wide * inverse_norm * gain[:, columns]).astype(jnp.bfloat16)
        cos, sin = cosine[:, span], sine[:, span]

        def dot(weight):
            return jnp.transpose(
                jnp.dot(normed[...], weight[...], preferred_element_type=jnp.float32)
            )

        def rotated(field, base, scale):
            for h in range(4):
                first = field[h * 96 : h * 96 + 48]
                second = field[h * 96 + 48 : h * 96 + 96]
                a = first * cos - second * sin
                b = second * cos + first * sin
                if scale is not None:
                    a, b = a * scale, b * scale
                out[h, base : base + 48, span] = a.astype(jnp.bfloat16)
                out[h, base + 48 : base + 96, span] = b.astype(jnp.bfloat16)

        rotated(dot(wk_v), 0, None)
        value = dot(wv_v)
        for h in range(4):
            out[h, 96:192, span] = value[h * 96 : h * 96 + 96].astype(jnp.bfloat16)
        rotated(dot(wq_v), 192, SCALE)

    def landed(dst, half, k):
        remote(dst, dst, hsend, hrecv, (half, k), sibling).wait_recv()

    def hand(src, dst, half, k, device):
        go(remote(src, dst, hsend, hrecv, (half, k), device))

    def lanes(half):
        return pl.ds(half * 256, 256)

    def piece(ref, i, half):
        return ref.at[i, :, lanes(half)]

    def from_out(d, base, size, half):
        return out.at[lax.rem(xi + d, 4), pl.ds(base, size), lanes(half)]

    def scatter(half):
        span = slice(half * 256, half * 256 + 256)
        hand(from_out(1, 0, 192, half), piece(own, xi, half), half, 1, at_x(1))
        hand(from_out(3, 0, 192, half), piece(own, xi, half), half, 2, at_x(3))
        hand(from_out(2, 0, 192, half), stage_x.at[pl.ds(0, 192), lanes(half)], half, 0, at_x(step))
        hand(from_out(0, 0, 192, half), piece(own1, xi, half), half, 12, above)
        hand(from_out(0, 0, 192, half), piece(sib, xi, half), half, 8, sibling)
        hand(from_out(1, 192, 96, half), piece(q, xi, half), half, 5, at_x(1))
        hand(from_out(3, 192, 96, half), piece(q, xi, half), half, 6, at_x(3))
        hand(from_out(2, 192, 96, half), stage_x.at[pl.ds(192, 96), lanes(half)], half, 4, at_x(step))
        own[xi, :, span] = out[xi, 0:192, span]
        q[xi, :, span] = out[xi, 192:288, span]

    def onward(half, k, d):
        source = lax.rem(xi + d, 4)
        landed(piece(own, source, half), half, k)
        hand(piece(own, source, half), piece(own1, source, half), half, 12 + d, above)
        hand(piece(own, source, half), piece(sib, source, half), half, 8 + d, sibling)

    def relay(half):
        origin = lax.rem(xi + 4 - step, 4)
        keys, queries = stage_x.at[pl.ds(0, 192), lanes(half)], stage_x.at[pl.ds(192, 96), lanes(half)]
        landed(keys, half, 0)
        hand(keys, piece(own, origin, half), half, 3, at_x(step))
        onward(half, 1, 3)
        onward(half, 2, 1)
        landed(queries, half, 4)
        hand(queries, piece(q, origin, half), half, 7, at_x(step))

    def share(half):
        for d in (0, 3, 1, 2):
            source = lax.rem(xi + d, 4)
            landed(piece(own1, source, half), half, 12 + d)
            hand(piece(own1, source, half), piece(sib1, source, half), half, 16 + d, sibling)

    def settle(half):
        for k, d in ((5, 3), (6, 1), (7, 2)):
            landed(piece(q, lax.rem(xi + d, 4), half), half, k)
        for d in range(4):
            landed(piece(sib, lax.rem(xi + d, 4), half), half, 8 + d)
            landed(piece(sib1, lax.rem(xi + d, 4), half), half, 16 + d)

    mine = pl.ds(pl.multiple_of(c * 192, 192), 192)

    def columns(d):
        return pl.ds(pl.multiple_of(lax.rem(y + d, 4) * 768, 768), 768)

    def weigh(src, dst, k, device):
        go(remote(src, dst, wsend, wrecv, k, device))

    def weight_came(dst, k):
        remote(dst, dst, wsend, wrecv, k, sibling).wait_recv()

    for half in (0, 1):
        even, odd = 2 * half, 2 * half + 1
        came(even, even, before).wait_recv()
        go(pass_on(even))
        came(4 + odd, odd, after).wait_recv()
        go(pass_on(odd))
        if half == 0:
            for n in (2, 3):
                go(to_right(n))
                go(to_left(n))
        else:
            relay(0)
            onward(0, 3, 2)
        came(odd, odd, before).wait_recv()
        came(4 + even, even, after).wait_recv()
        came(8 + even, even, lax.rem(y + 2, 4)).wait_recv()
        came(8 + odd, odd, lax.rem(y + 2, 4)).wait_recv()
        if half == 0:
            for copy in loads[1:6]:
                copy.wait()
        else:
            weigh(wout.at[mine, columns(2)], stage_y, 0, at_y(step))
            weigh(wout.at[mine, columns(1)], wo.at[y, mine], 1, right)
            weigh(wout.at[mine, columns(3)], wo.at[y, mine], 2, left)
        project(half)
        scatter(half)
    share(0)
    relay(1)
    weight_came(stage_y, 0)
    weigh(stage_y, wo.at[lax.rem(y + 4 - step, 4), mine], 3, at_y(step))
    onward(1, 3, 2)
    share(1)
    for n, d in ((1, 3), (2, 1), (3, 2)):
        source = lax.rem(y + d, 4)
        weight_came(wo.at[source, mine], n)
        weigh(wo.at[source, mine], wo.at[source, mine], 3 + d, sibling)
    settle(0)
    settle(1)
    other = pl.ds(pl.multiple_of((1 - c) * 192, 192), 192)
    for d in range(1, 4):
        weight_came(wo.at[lax.rem(y + d, 4), other], 3 + d)
    loads[6].wait()
    for copy in sent:
        copy.wait_send()


VM = pl.BlockSpec(memory_space=pltpu.VMEM)
ANY = pl.BlockSpec(memory_space=pl.ANY)
SM = pl.BlockSpec(memory_space=pltpu.SMEM)


def project(tokens, norm_gain, w_query, w_key, w_value, w_out, prompt_lengths):
    bf, f32 = jnp.bfloat16, jnp.float32
    return pl.pallas_call(
        project_kernel,
        name="project",
        out_shape=(
            jax.ShapeDtypeStruct((4, 288, 512), bf),
            *(jax.ShapeDtypeStruct((4, 192, 512), bf),) * 4,
            jax.ShapeDtypeStruct((4, 96, 512), bf),
            jax.ShapeDtypeStruct((4, 384, 768), bf),
        ),
        in_specs=[ANY] * 7,
        out_specs=[VM] * 7,
        scratch_shapes=[
            pltpu.SMEM((8,), jnp.int32),
            pltpu.VMEM((1, D), f32),
            pltpu.VMEM((4, 512, 768), bf),
            pltpu.VMEM((256, D), bf),
            pltpu.VMEM((D, 384), bf),
            pltpu.VMEM((D, 384), bf),
            pltpu.VMEM((D, 384), bf),
            pltpu.VMEM((48, 512), f32),
            pltpu.VMEM((48, 512), f32),
            pltpu.VMEM((288, 512), bf),
            pltpu.VMEM((192, 768), bf),
            pltpu.SemaphoreType.DMA((7,)),
            pltpu.SemaphoreType.DMA((12,)),
            pltpu.SemaphoreType.DMA((12,)),
            pltpu.SemaphoreType.DMA((2, 20)),
            pltpu.SemaphoreType.DMA((2, 20)),
            pltpu.SemaphoreType.DMA((7,)),
            pltpu.SemaphoreType.DMA((7,)),
        ],
        compiler_params=pltpu.CompilerParams(
            collective_id=1, has_side_effects=True, vmem_limit_bytes=52 << 20
        ),
    )(prompt_lengths, tokens, norm_gain.reshape(1, D), w_query, w_key, w_value, w_out)


def attend_kernel(planes, resume, *refs):
    lengths, q, *refs = refs
    pairs, refs = refs[: 2 * len(planes)], refs[2 * len(planes) :]
    if resume:
        acc_in, m_in, out, keys, values, query, acc, largest = refs
    else:
        acc_out, m_out, keys, values, query, acc, largest = refs
    s = lax.axis_index("seq")
    z, c = s // 8, lax.rem(s, 2)
    starts, total = starts_of(lengths)
    base = (z - planes[0]) * 4096
    filler = jnp.where(lax.broadcasted_iota(jnp.int32, (32, 512), 0) == 0, 1.0, 0.0)
    lead = 0 if resume else 3
    for k in range(lead):
        keys[k] = jnp.zeros((128, 512), jnp.bfloat16)
        values[k] = jnp.zeros((128, 512), jnp.bfloat16)
    for i in range(len(planes)):
        for b in range(4):
            for ref, k in ((pairs[2 * i], 2 * b + c), (pairs[2 * i + 1], 2 * b + 1 - c)):
                k = lead + 8 * i + k
                keys[k, 0:96] = ref[b, 0:96]
                keys[k, 96:128] = jnp.zeros((32, 512), jnp.bfloat16)
                values[k, 0:96] = ref[b, 96:192]
                values[k, 96:128] = filler.astype(jnp.bfloat16)

    def query_block(b, _):
        begin = (z * 8 + 2 * b + c) * 512
        wide = jnp.concatenate(
            [q[b].astype(jnp.float32), jnp.zeros((32, 512), jnp.float32)], axis=0
        )
        query[...] = jnp.transpose(wide).astype(jnp.bfloat16)
        if resume:
            acc[...] = acc_in[b]
            largest[...] = m_in[b]
        else:
            acc[...] = jnp.zeros_like(acc)
            largest[...] = jnp.full_like(largest, NEG)
        slots = begin + lax.broadcasted_iota(jnp.int32, (512, 1), 0)
        firsts = jnp.maximum(first_of(slots, starts), base)

        def visit(k, count, masked):
            halves = [slice(0, 256), slice(256, 512)]
            scores = [
                [
                    jnp.dot(query[half], keys[lead + k + i], preferred_element_type=jnp.float32)
                    for i in range(count)
                ]
                for half in halves
            ]
            for half, parts in zip(halves, scores):
                if masked:
                    at = base + k * 512 + lax.broadcasted_iota(jnp.int32, (1, 512), 1)
                    parts = [
                        jnp.where(
                            (at + i * 512 >= firsts[half]) & (at + i * 512 <= slots[half]),
                            part, NEG,
                        )
                        for i, part in enumerate(parts)
                    ]
                most = parts[0]
                for part in parts[1:]:
                    most = jnp.maximum(most, part)
                old = largest[half]
                new = jnp.maximum(old, jnp.max(most, axis=1, keepdims=True))
                sums = acc[half] * jnp.exp2(old - new)
                for i, part in enumerate(parts):
                    weights = jnp.exp2(part - new[:, 0:1]).astype(jnp.bfloat16)
                    sums = sums + lax.dot_general(
                        weights, values[lead + k + i], (((1,), (1,)), ((), ())),
                        preferred_element_type=jnp.float32,
                    )
                acc[half] = sums
                largest[half] = new

        low = first_of(begin, starts)
        high = first_of(jnp.minimum(begin + 511, total - 1), starts)
        if resume:
            start = jnp.clip((low - base) // 512, 0, 8)
            middle = jnp.clip((high - base + 511) // 512, start, 8)

            @pl.loop(start, middle)
            def _(k):
                visit(k, 1, True)

            @pl.loop(middle, 8)
            def _(k):
                visit(k, 1, False)

        else:
            top = 8 * len(planes) - 11 + 2 * b + c
            start = jnp.clip((low - base) // 512, 0, top + 3)
            middle = jnp.clip((high - base + 511) // 512, 0, top + 3)
            groups = (top + 7 - start) // 4
            clear = jnp.minimum(jnp.maximum(top - middle, 0) // 4, groups - 1)
            visit(top, 4, True)

            @pl.loop(1, clear + 1)
            def _(g):
                visit(top - 4 * g, 4, False)

            @pl.loop(clear + 1, groups)
            def _(g):
                visit(top - 4 * g, 4, True)

        if resume:
            result = jnp.where(slots < total, acc[...] / acc[:, 96:97], 0.0)
            out[b] = jnp.transpose(result)[0:96].astype(jnp.bfloat16)
        else:
            acc_out[b] = acc[...]
            m_out[b] = largest[...]
        return 0

    lax.fori_loop(0, 4, query_block, 0)


def attend(planes, prompt_lengths, q, blocks, state=()):
    bf, f32 = jnp.bfloat16, jnp.float32
    resume = len(state) > 0
    if resume:
        out_shape = jax.ShapeDtypeStruct((4, 96, 512), bf)
        out_specs = VM
    else:
        out_shape = (jax.ShapeDtypeStruct((4, 512, 128), f32),) * 2
        out_specs = [VM] * 2
    steps = 4 if resume else 13
    return pl.pallas_call(
        partial(attend_kernel, planes, resume),
        name="attend_far" if resume else "attend_near",
        out_shape=out_shape,
        in_specs=[SM] + [VM] * (1 + len(blocks) + len(state)),
        out_specs=out_specs,
        scratch_shapes=[
            pltpu.VMEM((8 * len(planes) + (0 if resume else 3), 128, 512), bf),
            pltpu.VMEM((8 * len(planes) + (0 if resume else 3), 128, 512), bf),
            pltpu.VMEM((512, 128), bf),
            pltpu.VMEM((512, 128), f32),
            pltpu.VMEM((512, 128), f32),
        ],
        compiler_params=pltpu.CompilerParams(vmem_limit_bytes=24 << 20),
        cost_estimate=pl.CostEstimate(
            flops=4 * steps * 4 * 512 * 512 * 256, bytes_accessed=8 << 20,
            transcendentals=4 * steps * 512 * 512,
        ),
    )(prompt_lengths, q, *blocks, *state)


def finish_kernel(
    ot, wo, tokens, request_slots, gain, vocab, hidden, norm_out, top_out,
    att, total, rows, vpad, buf1, acc1, buf2, chunk, full, part, sq, partr, sqr, mine,
    buf5, buf6, fin, send, recv, tsend, trecv,
):
    s, y = lax.axis_index("seq"), lax.axis_index("tp")
    z, p = s // 8, lax.rem(s, 8)
    x, c = p // 2, lax.rem(p, 2)

    def at_x(d):
        return (z * 8 + lax.rem(x + d, 4) * 2 + c, y)

    def peer_z(d):
        return (lax.rem(z + d, 8) * 8 + p, y)

    def peer_p(d):
        return (z * 8 + lax.rem(p + d, 8), y)

    def peer_y(d):
        return (s, lax.rem(y + d, 4))

    right, left = peer_y(1), peer_y(3)
    before, after = lax.rem(y + 3, 4), lax.rem(y + 1, 4)
    greet(
        [peer_p(d) for d in range(1, 8)]
        + [peer_y(d) for d in range(1, 4)]
        + [peer_z(d) for d in range(1, 8)]
    )
    sent = []

    def go(*args):
        copy = remote(*args)
        copy.start()
        sent.append(copy)

    def came(dst, k):
        remote(dst, dst, send, recv, k, right).wait_recv()

    for d in (2, 1, 3):
        go(ot.at[lax.rem(x + d, 4)], att.at[y, x], send, recv, d, at_x(d))
    att[y, x] = ot[x]
    head = [lax.rem(x + 4 - d, 4) for d in range(4)]
    for d in (0, 1, 3, 2):
        if d == 0:
            piece = ot.at[x]
        else:
            piece = att.at[y, head[d]]
            came(piece, d)
        go(piece, att.at[y, head[d]], send, recv, 4 + d, right)
        go(piece, att.at[y, head[d]], send, recv, 8 + d, left)
    picks = (
        request_slots[...] == s * 512 + lax.broadcasted_iota(jnp.int32, (512, 128), 0)
    ).astype(jnp.bfloat16)
    columns = vocab.shape[0]
    vpad[496:512] = jnp.zeros((16, 768), jnp.bfloat16)
    vpad[0:columns] = vocab[...]

    def term(group):
        return lax.dot_general(
            att[group].reshape(384, 512), wo[group], (((0,), (0,)), ((), ())),
            preferred_element_type=jnp.float32,
        ).astype(jnp.bfloat16).astype(jnp.float32)

    total[...] = tokens[...].astype(jnp.float32) + term(y)
    for d in (0, 1):
        came(att.at[before, head[d]], 4 + d)
        go(att.at[before, head[d]], att.at[before, head[d]], send, recv, 12 + d, right)
    for d in (3, 2):
        came(att.at[after, head[d]], 8 + d)
        go(att.at[after, head[d]], att.at[after, head[d]], send, recv, 12 + d, left)
    for d in (3, 2):
        came(att.at[before, head[d]], 4 + d)
    total[...] += term(before)
    for d in (0, 1):
        came(att.at[after, head[d]], 8 + d)
    total[...] += term(after)
    across = lax.rem(y + 2, 4)
    for d in range(4):
        came(att.at[across, head[d]], 12 + d)
    result = (total[...] + term(across)).astype(jnp.bfloat16)
    hidden[...] = result
    rows[...] = lax.dot_general(
        picks, result, (((0,), (0,)), ((), ())), preferred_element_type=jnp.float32
    ).astype(jnp.bfloat16).reshape(8, 16, 768)

    def exchange(phase, count, peer, src, dst, landed=None):
        arrivals = []
        for d in range(1, count):
            copy = remote(src(d), dst(d), tsend, trecv, (phase, d), peer(d))
            copy.start()
            sent.append(copy)
            where = dst(d) if landed is None else landed(d)
            arrivals.append(remote(src(d), where, tsend, trecv, (phase, d), peer(d)))
        return arrivals

    def arrive(copies):
        for copy in copies:
            copy.wait_recv()

    arrive(exchange(
        0, 8, peer_p, lambda d: rows.at[lax.rem(p + d, 8)], lambda d: buf1.at[d - 1]
    ))
    mix = rows[p].astype(jnp.float32)
    for d in range(7):
        mix = mix + buf1[d].astype(jnp.float32)
    acc1[...] = mix.astype(jnp.bfloat16)
    arrive(exchange(1, 8, peer_z, lambda d: acc1, lambda d: buf2.at[d - 1]))
    for d in range(7):
        mix = mix + buf2[d].astype(jnp.float32)
    chunk[...] = mix.astype(jnp.bfloat16)
    copies = exchange(
        2, 8, peer_p, lambda d: chunk, lambda d: full.at[p],
        lambda d: full.at[lax.rem(p + 8 - d, 8)],
    )
    full[p] = chunk[...]
    arrive(copies)
    wide = full[...].astype(jnp.float32).reshape(REQS, 768)
    squares = jnp.sum(wide * wide, axis=1, keepdims=True)
    scaled = wide * gain[...]
    high = scaled.astype(jnp.bfloat16)
    low = (scaled - high.astype(jnp.float32)).astype(jnp.bfloat16)

    def against_vocab(a):
        return lax.dot_general(
            a, vpad[...], (((1,), (1,)), ((), ())), preferred_element_type=jnp.float32
        )

    part[...] = (against_vocab(high) + against_vocab(low)).astype(jnp.bfloat16).reshape(4, 32, 512)
    sq[...] = jnp.broadcast_to(squares, (REQS, 128)).reshape(4, 32, 128)
    copies = exchange(3, 4, peer_y, lambda d: part.at[lax.rem(y + d, 4)], lambda d: partr.at[d - 1])
    copies += exchange(4, 4, peer_y, lambda d: sq.at[lax.rem(y + d, 4)], lambda d: sqr.at[d - 1])
    arrive(copies)
    summed = part[y].astype(jnp.float32)
    square = sq[y]
    for d in range(3):
        summed = summed + partr[d].astype(jnp.float32)
        square = square + sqr[d]
    column = lax.broadcasted_iota(jnp.int32, (32, 512), 1)
    best = jnp.max(jnp.where(column < columns, summed, -jnp.inf), axis=1, keepdims=True)
    norm = jnp.sqrt(square / D + 1e-05)
    best = jnp.broadcast_to(best, (32, 128)) / norm
    fin[y, 0] = jnp.transpose(norm)[0:8, :]
    mine[0] = jnp.transpose(best)[0:8, :]
    arrive(exchange(5, 8, peer_p, lambda d: mine.at[0], lambda d: buf5.at[d - 1]))
    top = mine[0]
    for d in range(7):
        top = jnp.maximum(top, buf5[d])
    mine[1] = top
    arrive(exchange(6, 8, peer_z, lambda d: mine.at[1], lambda d: buf6.at[d - 1]))
    for d in range(7):
        top = jnp.maximum(top, buf6[d])
    fin[y, 1] = top
    arrive(exchange(
        7, 4, peer_y, lambda d: fin.at[y], lambda d: fin.at[y],
        lambda d: fin.at[lax.rem(y + 4 - d, 4)],
    ))
    norm_out[...] = jnp.concatenate([fin[i, 0, 0:1] for i in range(4)], axis=1)
    top_out[...] = jnp.concatenate([fin[i, 1, 0:1] for i in range(4)], axis=1)
    for copy in sent:
        copy.wait_send()


def finish(ot, wo, tokens, request_slots, final_gain, w_vocab):
    bf, f32 = jnp.bfloat16, jnp.float32
    hidden, norm, top = pl.pallas_call(
        finish_kernel,
        name="finish",
        out_shape=(
            jax.ShapeDtypeStruct((512, 768), bf),
            jax.ShapeDtypeStruct((1, REQS), f32),
            jax.ShapeDtypeStruct((1, REQS), f32),
        ),
        in_specs=[VM] * 6,
        out_specs=[VM] * 3,
        scratch_shapes=[
            pltpu.VMEM((4, 4, 96, 512), bf),
            pltpu.VMEM((512, 768), f32),
            pltpu.VMEM((8, 16, 768), bf),
            pltpu.VMEM((512, 768), bf),
            pltpu.VMEM((7, 16, 768), bf),
            pltpu.VMEM((16, 768), bf),
            pltpu.VMEM((7, 16, 768), bf),
            pltpu.VMEM((16, 768), bf),
            pltpu.VMEM((8, 16, 768), bf),
            pltpu.VMEM((4, 32, 512), bf),
            pltpu.VMEM((4, 32, 128), f32),
            pltpu.VMEM((3, 32, 512), bf),
            pltpu.VMEM((3, 32, 128), f32),
            pltpu.VMEM((2, 8, 32), f32),
            pltpu.VMEM((7, 8, 32), f32),
            pltpu.VMEM((7, 8, 32), f32),
            pltpu.VMEM((4, 2, 8, 32), f32),
            pltpu.SemaphoreType.DMA((16,)),
            pltpu.SemaphoreType.DMA((16,)),
            pltpu.SemaphoreType.DMA((8, 8)),
            pltpu.SemaphoreType.DMA((8, 8)),
        ],
        compiler_params=pltpu.CompilerParams(
            collective_id=3, has_side_effects=True, vmem_limit_bytes=32 << 20
        ),
    )(ot, wo, tokens, request_slots.reshape(1, REQS), final_gain.reshape(1, 768), w_vocab.T)
    return hidden, norm.reshape(REQS), top.reshape(REQS)


def along_z(array):
    return lax.ppermute(array, "seq", [(i, i + 8) for i in range(56)])


def across_chip(array):
    return lax.ppermute(array, "seq", [(i, i ^ 1) for i in range(64)])


def shards(
    tokens, norm_gain, w_query, w_key, w_value, w_out, final_gain, w_vocab,
    segment_ids, prompt_lengths, request_slots,
):
    qkv, own, sib, own1, sib1, q, wo = project(
        tokens, norm_gain, w_query, w_key, w_value, w_out, prompt_lengths
    )
    kv_cache = jnp.transpose(qkv[:, :192], (0, 2, 1))
    own2 = along_z(own1)
    state = attend((1, 0), prompt_lengths, q, (own1, sib1, own, sib))
    own2, *state = lax.optimization_barrier((own2, *state))
    sib2 = across_chip(own2)
    ot = attend((2,), prompt_lengths, q, (own2, sib2), state)
    hidden, hidden_norm, top_logit = finish(
        ot, wo, tokens, request_slots, final_gain, w_vocab
    )
    return (kv_cache, hidden, hidden_norm, top_logit)


def solution(mesh):
    return jax.shard_map(
        shards,
        mesh=mesh,
        in_specs=(
            P("seq", "tp"),
            P(),
            P(None, "tp"),
            P(None, "tp"),
            P(None, "tp"),
            P("tp", None),
            P("tp"),
            P("tp", "seq"),
            P("seq"),
            P(),
            P(),
        ),
        out_specs=(P("tp", "seq", None), P("seq", "tp"), P(), P()),
        check_vma=False,
    )
```
